512 devices in a mesh: feeder: 32 (over x, y, core), scen: 16 (over z).
Axes of the slice: x: 4, y: 4, z: 16, core: 2. Of those that a mesh axis runs over, the one named last changes fastest.
Arguments:
- anchor: bfloat16 [256, 24, 16384], P('scen', None, 'feeder'), may hold values from -6 to 6
- cost_lin: bfloat16 [256, 24, 16384], P('scen', None, 'feeder'), may hold values from -6 to 6
- dual: float32 [256, 24, 16384], P('scen', None, 'feeder'), may hold values from -4 to 4
- target: float32 [256, 24], P('scen'), may hold values from -4 to 4
- leaf_weight: float32 [256], P('scen'), may hold values from 1 to 10
- q_mat: bfloat16 [16384, 512], P('feeder'), may hold values from -0.25 to 0.25
- diag_gain: float32 [16384], P('feeder'), may hold values from 0.5 to 2
- block_mask: int32 [32, 4, 4], P('feeder'), may hold values from 0 to 1, as said below
- ancestor: int32 [24, 256], P(None, 'scen'), may hold values from 0 to 255, as said below
Outputs:
- setpoints: float32 [256, 24, 16384], P('scen', None, 'feeder')
- average: float32 [256, 24, 16384], P('scen', None, 'feeder')
- new_dual: float32 [256, 24, 16384], P('scen', None, 'feeder')
The draws below stay inside these ranges and needn't reach their ends.
Inputs may be any that keep to these rules, and one draw needn't show every extreme that they name: `block_mask`: every diagonal block is present; the share of present off-diagonal blocks differs from feeder to feeder. ancestor[t, s] is the first leaf of the section-t tree node that holds leaf s: the leaves of a node are consecutive, ancestor[0, s] = 0, and every section-t node lies inside one section-(t-1) node. Nodes may span several groups at any section.
All inputs are finite; a program needn't handle non-finite values.
Results may differ from the reference program's by a relative error of at most 0.0003.
Values sent between devices are 32-bit elements; how exact they have to be, the bound alone decides.
No kernel may reach another device: no remote copies, remote signals or barrier semaphores. Data moves between devices by JAX's collectives and lax.ppermute only.
A program may use at most 64 MiB of HBM per device.

```python
import math
import jax
import jax.numpy as jnp
from jax import lax

NODES = 512
BLOCK = 128
SECTIONS = 24
PROX_ITERS = 8
NBLK = 4
FEEDERS = 32
SCEN = 256


def draw_block_mask(key, part):
    density = jax.random.randint(jax.random.fold_in(key, 11), (FEEDERS, 1, 1), 0, 4)
    rolls = jax.random.randint(jax.random.fold_in(key, 12), (FEEDERS, NBLK, NBLK), 0, 4)
    present = (rolls < density).astype(jnp.int32)
    diagonal = jnp.eye(NBLK, dtype=jnp.int32)[None, :, :]
    return jnp.maximum(present, diagonal)


def draw_ancestor(key, part):
    appear = jax.random.randint(jax.random.fold_in(key, 21), (SCEN,), 1, 2 * SECTIONS)
    leaf_ids = jnp.arange(SCEN, dtype=jnp.int32)
    appear = jnp.where(leaf_ids == SCEN - 1, SECTIONS - 1, appear)
    section_ids = jnp.arange(SECTIONS, dtype=jnp.int32)[:, None]
    starts = jnp.where((appear[None, :] <= section_ids) | (leaf_ids[None, :] == 0), leaf_ids[None, :], 0)
    return lax.cummax(starts, axis=1).astype(jnp.int32)


def block_levels(own_key, dims, pieces, smallest, high):
    def one(axis_at, shards_of):
        draws = jax.random.uniform(jax.random.fold_in(jax.random.fold_in(own_key, 6), axis_at), (shards_of,), jnp.float32, smallest / len(pieces), high / len(pieces))
        return jnp.repeat(jnp.exp(draws), dims[axis_at] // shards_of).reshape((-1,) + (1,) * (len(dims) - axis_at - 1))

    factor_of = one(*pieces[0])
    for cut in pieces[1:]:
        factor_of = factor_of * one(*cut)
    return factor_of


def scatter_about(own_key, shape, scale, limit, shards=(), held_as=jnp.bfloat16):
    factor_of = block_levels(own_key, shape, shards, -0.22, 0.18) if shards else 1.0
    result = jax.random.normal(own_key, shape, jnp.float32) * scale * factor_of
    return jnp.minimum(jnp.maximum(result, -limit), limit).astype(held_as)


def setup_inputs(seed: int = 0) -> dict:
    seeds = jax.random.split(jax.random.key(seed), 10)
    anchor = scatter_about(seeds[0], (SCEN, SECTIONS, FEEDERS * NODES), 1.0, 6.0, ((0, 16), (2, 32)))
    cost_lin = scatter_about(seeds[1], (SCEN, SECTIONS, FEEDERS * NODES), 1.0, 6.0, ((0, 16), (2, 32)))
    dual = scatter_about(seeds[2], (SCEN, SECTIONS, FEEDERS * NODES), 0.5, 4.0, ((0, 16), (2, 32)), jnp.float32)
    target = scatter_about(seeds[3], (SCEN, SECTIONS), 1.0, 4.0, ((0, 16),), jnp.float32)
    leaf_weight = jnp.clip(jnp.exp(math.log(10.0) - 2.3025851 * jax.random.uniform(seeds[4], (SCEN,), jnp.float32) ** block_levels(seeds[4], (SCEN,), ((0, 16),), -0.2, 0.2)), 1.0, 10.0)
    q_mat = scatter_about(seeds[5], (FEEDERS * NODES, NODES), NODES ** -0.5, 0.25, ((0, 32),))
    diag_gain = jnp.clip(jnp.exp(math.log(2.0) - 1.3862944 * jax.random.uniform(seeds[6], (FEEDERS * NODES,), jnp.float32) ** block_levels(seeds[6], (FEEDERS * NODES,), ((0, 32),), -0.2, 0.2)), 0.5, 2.0)
    block_mask = draw_block_mask(jax.random.fold_in(seeds[9], 71), 0)
    ancestor = draw_ancestor(jax.random.fold_in(seeds[9], 71), 0)
    return dict(anchor=anchor, cost_lin=cost_lin, dual=dual, target=target, leaf_weight=leaf_weight, q_mat=q_mat, diag_gain=diag_gain, block_mask=block_mask, ancestor=ancestor)


penalty = 1.0
step_size = 0.08
coupling = 4.0
power_limit = 2.0


def reference(anchor, cost_lin, dual, target, leaf_weight, q_mat, diag_gain, block_mask, ancestor):
    width_all = FEEDERS * NODES
    expand = jnp.repeat(jnp.repeat(block_mask, BLOCK, axis=1), BLOCK, axis=2)
    q_eff = q_mat.reshape(FEEDERS, NODES, NODES).astype(jnp.float32) * expand.astype(jnp.float32)
    start_pt = anchor.astype(jnp.float32)
    state = start_pt
    for sweep in range(PROX_ITERS):
        flat = state.reshape(SCEN * SECTIONS, FEEDERS, NODES).astype(jnp.bfloat16).astype(jnp.float32)
        image = jnp.einsum('rfn,fnm->rfm', flat, q_eff).reshape(SCEN, SECTIONS, width_all)
        head = jnp.sum(state, axis=2) / width_all
        grad = image + 2.0 * diag_gain * state + cost_lin.astype(jnp.float32) + dual
        grad = grad + penalty * (state - start_pt) + coupling * (head - target)[:, :, None]
        state = jnp.clip(state - step_size * grad, -power_limit, power_limit)
    weighted = leaf_weight[:, None, None] * state
    section_avgs = []
    for section in range(SECTIONS):
        owners = ancestor[section]
        sums = jax.ops.segment_sum(weighted[:, section, :], owners, num_segments=SCEN)
        weights = jax.ops.segment_sum(leaf_weight, owners, num_segments=SCEN)
        section_avgs.append(sums[owners] / weights[owners][:, None])
    average = jnp.stack(section_avgs, axis=1)
    new_dual = dual + penalty * (state - average)
    return state, average, new_dual
```

```python
import jax
import jax.numpy as jnp
from jax import lax
from jax.sharding import PartitionSpec as P

PROX_ITERS = 8


penalty = 1.0
step_size = 0.08
coupling = 4.0
power_limit = 2.0


def feeder_sum(part, feeders):
    spread = jnp.broadcast_to(part, (feeders,) + part.shape)
    return jnp.sum(lax.all_to_all(spread, "feeder", 0, 0), axis=0)


def local(anchor, cost_lin, dual, target, leaf_weight, q_mat, diag_gain, block_mask, ancestor):
    leaves, sections, nodes = anchor.shape
    rows = leaves * sections
    count = block_mask.shape[1]
    width = nodes // count
    feeders = lax.axis_size("feeder")
    groups = lax.axis_size("scen")
    total_nodes = feeders * nodes
    highest = lax.Precision.HIGHEST
    start_pt = anchor.astype(jnp.float32)
    fixed_part = cost_lin.astype(jnp.float32) + dual - penalty * start_pt
    diag_term = 2.0 * diag_gain + penalty
    expand = jnp.repeat(jnp.repeat(block_mask[0], width, axis=0), width, axis=1).astype(
        jnp.bfloat16
    )
    q_eff = q_mat * expand
    state = start_pt
    for sweep in range(PROX_ITERS):
        flat = state.reshape(rows, nodes).astype(jnp.bfloat16)
        image = jnp.dot(flat, q_eff, preferred_element_type=jnp.float32)
        part = jnp.sum(state, axis=2).reshape(rows // 128, 128)
        head = feeder_sum(part, feeders).reshape(leaves, sections) / total_nodes
        grad = image.reshape(leaves, sections, nodes) + diag_term * state + fixed_part
        grad = grad + coupling * (head - target)[:, :, None]
        state = jnp.clip(state - step_size * grad, -power_limit, power_limit)

    first_leaf = lax.axis_index("scen") * leaves
    same = (ancestor[:, :, None] == ancestor[:, None, :]).astype(jnp.float32)
    weighted = leaf_weight[:, None, None] * state
    own_sum = jnp.einsum("tlr,rtn->ltn", same, weighted, precision=highest)
    own_weight = jnp.einsum("tlr,r->lt", same, leaf_weight, precision=highest)
    continued = (ancestor[:, 0] < first_leaf).astype(jnp.float32)
    spanning = (ancestor[:, leaves - 1] < first_leaf).astype(jnp.float32)
    tail_sum, tail_weight = own_sum[leaves - 1], own_weight[leaves - 1]
    head_sum, head_weight = own_sum[0] * continued[:, None], own_weight[0] * continued

    node_blocks = nodes // 128
    section_blocks = groups // node_blocks
    per = sections // section_blocks

    def to_owner(sums):
        cut = sums.reshape(section_blocks, per, node_blocks, 128)
        return cut.transpose(0, 2, 1, 3).reshape(groups, per, 128)

    scalars = jnp.stack([tail_weight, head_weight, spanning], axis=0)
    scalars = scalars.reshape(3, section_blocks, per).transpose(1, 0, 2)
    scalars = jnp.pad(scalars, ((0, 0), (0, 0), (0, 128 - per)))
    scalars = jnp.repeat(scalars, node_blocks, axis=0)
    sent = jnp.concatenate([to_owner(tail_sum), to_owner(head_sum), scalars], axis=1)
    got = lax.all_to_all(sent, "scen", 0, 0)
    tails, heads = got[:, :per], got[:, per : 2 * per]
    tail_w, head_w, span = (got[:, 2 * per + i, :per] for i in range(3))

    ids = jnp.arange(groups)
    between = (ids[None, None, :] > ids[:, None, None]) & (ids[None, None, :] < ids[None, :, None])
    broken = jnp.any(between[:, :, :, None] & (span[None, None, :, :] < 0.5), axis=2)
    upper = (ids[:, None] < ids[None, :])[:, :, None]
    link = jnp.where(upper & ~broken, 1.0, 0.0)
    before = jnp.sum(link[:, :, :, None] * tails[:, None], axis=0)
    after = jnp.sum(link[:, :, :, None] * heads[None, :], axis=1)
    before_w = jnp.sum(link * tail_w[:, None], axis=0)
    after_w = jnp.sum(link * head_w[None, :], axis=1)
    first_w = before_w + head_w + span * after_w
    last_w = tail_w + after_w + span * before_w
    span_n = span[:, :, None]
    first_avg = (before + heads + span_n * after) / first_w[:, :, None]
    last_avg = (tails + after + span_n * before) / last_w[:, :, None]
    back = lax.all_to_all(jnp.concatenate([first_avg, last_avg], axis=1), "scen", 0, 0)

    def from_owner(chunk):
        cut = chunk.reshape(section_blocks, node_blocks, per, 128)
        return cut.transpose(0, 2, 1, 3).reshape(sections, nodes)

    first_avg, last_avg = from_owner(back[:, :per]), from_owner(back[:, per:])
    in_last = (ancestor == ancestor[:, leaves - 1 :]).T[:, :, None]
    in_front = (ancestor < first_leaf).T[:, :, None]
    average = own_sum / own_weight[:, :, None]
    average = jnp.where(in_last, last_avg[None], jnp.where(in_front, first_avg[None], average))
    new_dual = dual + penalty * (state - average)
    return (state, average, new_dual)


def solution(mesh):
    return jax.shard_map(
        local,
        mesh=mesh,
        in_specs=(
            P("scen", None, "feeder"),
            P("scen", None, "feeder"),
            P("scen", None, "feeder"),
            P("scen", None),
            P("scen"),
            P("feeder", None),
            P("feeder"),
            P("feeder", None, None),
            P(None, "scen"),
        ),
        out_specs=(P("scen", None, "feeder"), P("scen", None, "feeder"), P("scen", None, "feeder")),
    )
```

```python
import jax
import jax.numpy as jnp
from jax import lax
from jax.experimental import pallas as pl
from jax.experimental.pallas import tpu as pltpu
from jax.sharding import PartitionSpec as P

PROX_ITERS = 8
LANES = 128


penalty = 1.0
step_size = 0.08
coupling = 4.0
power_limit = 2.0

VMEM = pl.BlockSpec(memory_space=pltpu.VMEM)
SMEM = pl.BlockSpec(memory_space=pltpu.SMEM)
HBM = pl.BlockSpec(memory_space=pl.ANY)
PARAMS = pltpu.CompilerParams(vmem_limit_bytes=12 * 1024 * 1024)


def row_sums(block):
    total = block[:, :LANES]
    for start in range(LANES, block.shape[1], LANES):
        total = total + block[:, start : start + LANES]
    return jnp.sum(total.T, axis=0, keepdims=True)


def sum_kernel(anchor_ref, sums_ref):
    for i in range(anchor_ref.shape[0] // LANES):
        block = anchor_ref[i * LANES : (i + 1) * LANES, :].astype(jnp.float32)
        sums_ref[i : i + 1, :] = row_sums(block)


def affine(x, image, gain, fixed):
    return x * gain - (fixed + step_size * image)


def prep_kernel(
    first_ref, weight_ref, mask_ref, anchor_ref, cost_ref, dual_ref, q_ref, diag_ref, anc_ref,
    q_out, fixed_out, z_out, gain_out, same_out, recip_out, pick_out, cont_out, scalar_out,
):
    nodes = q_ref.shape[0]
    count = mask_ref.shape[0]
    width = nodes // count
    for i in range(count):
        for j in range(count):
            rows, cols = slice(i * width, (i + 1) * width), slice(j * width, (j + 1) * width)
            keep = mask_ref[i, j].astype(jnp.float32).astype(jnp.bfloat16)
            q_out[rows, cols] = q_ref[rows, cols] * keep
    gain = 1.0 - step_size * (2.0 * diag_ref[...] + penalty)
    gain_out[...] = gain
    start_pt = anchor_ref[...].astype(jnp.float32)
    fixed = step_size * (cost_ref[...].astype(jnp.float32) + dual_ref[...] - penalty * start_pt)
    fixed_out[...] = fixed
    image = jnp.dot(anchor_ref[...], q_out[...], preferred_element_type=jnp.float32)
    z_out[...] = affine(start_pt, image, gain, fixed)

    leaves = weight_ref.shape[0]
    sections = anc_ref.shape[0] // leaves
    first_leaf = first_ref[0]
    anc = [anc_ref[i * sections : (i + 1) * sections, :] for i in range(leaves)]
    run = []
    for i in range(leaves):
        rows = slice(i * sections, (i + 1) * sections)
        weight = jnp.full(anc[0].shape, weight_ref[i], jnp.float32)
        if i == 0:
            same = jnp.zeros(anc[0].shape, jnp.float32)
            run.append(weight)
        else:
            same = jnp.where(anc[i] == anc[i - 1], 1.0, 0.0)
            run.append(weight + same * run[-1])
        same_out[rows, :] = same
    for i in reversed(range(leaves - 1)):
        run[i] = jnp.where(anc[i + 1] == anc[i], run[i + 1], run[i])
    for i in range(leaves):
        rows = slice(i * sections, (i + 1) * sections)
        recip_out[rows, :] = 1.0 / run[i]
        front = jnp.where(anc[i] < first_leaf, 1.0, 0.0)
        pick_out[rows, :] = jnp.where(anc[i] == anc[-1], 2.0, front)
    cont = jnp.where(anc[0] < first_leaf, 1.0, 0.0)
    span = jnp.where(anc[-1] < first_leaf, 1.0, 0.0)
    cont_out[...] = cont
    lane = lax.broadcasted_iota(jnp.int32, anc[0].shape, 1)
    scalar_out[...] = jnp.where(lane == 0, run[-1], jnp.where(lane == 1, run[0] * cont, span))


def clipped(total_nodes, got_ref, target_ref, z_ref, x_ref):
    parts = jnp.sum(got_ref[...], axis=0)
    shift = (step_size * coupling) * (parts * (1.0 / total_nodes) - target_ref[...])
    for i in range(z_ref.shape[0] // LANES):
        rows = slice(i * LANES, (i + 1) * LANES)
        tile = jnp.broadcast_to(shift[i : i + 1, :], (LANES, LANES)).T
        for start in range(0, z_ref.shape[1], LANES):
            cols = slice(start, start + LANES)
            x_ref[rows, cols] = jnp.clip(z_ref[rows, cols] - tile, -power_limit, power_limit)


def step_kernel(
    total_nodes, got_ref, target_ref, z_ref, q_ref, fixed_ref, gain_ref, sums_ref, z_out, x_ref
):
    clipped(total_nodes, got_ref, target_ref, z_ref, x_ref)
    for i in range(x_ref.shape[0] // LANES):
        sums_ref[i : i + 1, :] = row_sums(x_ref[i * LANES : (i + 1) * LANES, :])
    x = x_ref[...]
    image = jnp.dot(x.astype(jnp.bfloat16), q_ref[...], preferred_element_type=jnp.float32)
    z_out[...] = affine(x, image, gain_ref[...], fixed_ref[...])


def last_kernel(
    total_nodes, weight_ref, got_ref, target_ref, z_ref, same_ref, recip_ref, cont_ref, scalar_ref,
    x_ref, own_ref, sent_ref, tail_ref, head_ref,
):
    clipped(total_nodes, got_ref, target_ref, z_ref, x_ref)
    leaves = weight_ref.shape[0]
    sections = cont_ref.shape[0]
    nodes = x_ref.shape[1]
    owners = sent_ref.shape[0]
    node_blocks = nodes // LANES
    per = sections * node_blocks // owners
    for start in range(0, nodes, LANES):
        cols = slice(start, start + LANES)
        run = []
        for i in range(leaves):
            rows = slice(i * sections, (i + 1) * sections)
            term = weight_ref[i] * x_ref[rows, cols]
            run.append(term if i == 0 else term + same_ref[rows, :] * run[-1])
        total = run[-1]
        tail_ref[:, cols] = total
        for i in reversed(range(leaves)):
            rows = slice(i * sections, (i + 1) * sections)
            if i < leaves - 1:
                later = slice((i + 1) * sections, (i + 2) * sections)
                total = jnp.where(same_ref[later, :] > 0.5, total, run[i])
            own_ref[rows, cols] = total * recip_ref[rows, :]
        head_ref[:, cols] = total * cont_ref[...]
    zeros = jnp.zeros((8 - per, LANES), jnp.float32)
    for owner in range(owners):
        block, col = owner // node_blocks, owner % node_blocks
        rows, cols = slice(block * per, (block + 1) * per), slice(col * LANES, (col + 1) * LANES)
        sent_ref[owner, 0:per, :] = tail_ref[rows, cols]
        sent_ref[owner, per:8, :] = zeros
        sent_ref[owner, 8 : 8 + per, :] = head_ref[rows, cols]
        sent_ref[owner, 8 + per : 16, :] = zeros
        sent_ref[owner, 16 : 16 + per, :] = scalar_ref[rows, :]
        sent_ref[owner, 16 + per : 24, :] = zeros


def owner_kernel(got_ref, back_ref):
    groups = got_ref.shape[0]
    shape = (8, LANES)
    tails = [got_ref[g, 0:8, :] for g in range(groups)]
    heads = [got_ref[g, 8:16, :] for g in range(groups)]
    scalars = [got_ref[g, 16:24, :] for g in range(groups)]
    spans = [jnp.broadcast_to(s[:, 2:3], shape) for s in scalars]
    tail_w = [jnp.broadcast_to(s[:, 0:1], shape) for s in scalars]
    head_w = [jnp.broadcast_to(s[:, 1:2], shape) for s in scalars]
    zero = jnp.zeros(shape, jnp.float32)
    before, before_w, after, after_w = [zero], [zero], [zero], [zero]
    for g in range(groups - 1):
        before.append(tails[g] + spans[g] * before[-1])
        before_w.append(tail_w[g] + spans[g] * before_w[-1])
    for g in reversed(range(1, groups)):
        after.insert(0, heads[g] + spans[g] * after[0])
        after_w.insert(0, head_w[g] + spans[g] * after_w[0])
    for g in range(groups):
        first_w = before_w[g] + head_w[g] + spans[g] * after_w[g]
        last_w = tail_w[g] + after_w[g] + spans[g] * before_w[g]
        first_w = jnp.where(first_w > 0.0, first_w, 1.0)
        last_w = jnp.where(last_w > 0.0, last_w, 1.0)
        back_ref[g, 0:8, :] = (before[g] + heads[g] + spans[g] * after[g]) / first_w
        back_ref[g, 8:16, :] = (tails[g] + after[g] + spans[g] * before[g]) / last_w


def final_kernel(
    got_ref, own_ref, pick_ref, x_ref, dual_ref, average_hbm, new_dual_hbm,
    first_ref, last_ref, average_ref, new_dual_ref, sems,
):
    owners = got_ref.shape[0]
    sections, nodes = first_ref.shape
    node_blocks = nodes // LANES
    per = sections * node_blocks // owners
    for owner in range(owners):
        block, col = owner // node_blocks, owner % node_blocks
        rows, cols = slice(block * per, (block + 1) * per), slice(col * LANES, (col + 1) * LANES)
        first_ref[rows, cols] = got_ref[owner, 0:per, :]
        last_ref[rows, cols] = got_ref[owner, 8 : 8 + per, :]
    leaves = x_ref.shape[0] // sections
    chunks = sems.shape[1]
    each = leaves // chunks
    copies = []
    for chunk in range(chunks):
        for i in range(chunk * each, (chunk + 1) * each):
            rows = slice(i * sections, (i + 1) * sections)
            pick = pick_ref[rows, :]
            for start in range(0, nodes, LANES):
                cols = slice(start, start + LANES)
                ends = jnp.where(pick > 1.5, last_ref[:, cols], first_ref[:, cols])
                average = jnp.where(pick > 0.5, ends, own_ref[rows, cols])
                average_ref[rows, cols] = average
                new_dual_ref[rows, cols] = dual_ref[rows, cols] + penalty * (
                    x_ref[rows, cols] - average
                )
        part = pl.ds(chunk * each * sections, each * sections)
        for n, (src, dst) in enumerate(((average_ref, average_hbm), (new_dual_ref, new_dual_hbm))):
            copy = pltpu.make_async_copy(src.at[part, :], dst.at[part, :], sems.at[n, chunk])
            copy.start()
            copies.append(copy)
    for copy in copies:
        copy.wait()


def call(kernel, inputs, outputs, in_specs=None, out_specs=None, scratch=(), name=None):
    return pl.pallas_call(
        kernel,
        out_shape=outputs,
        in_specs=in_specs or [VMEM] * len(inputs),
        out_specs=out_specs or jax.tree.map(lambda _: VMEM, outputs),
        scratch_shapes=scratch,
        compiler_params=PARAMS,
        name=name,
    )(*inputs)


def shaped(shape, dtype=jnp.float32):
    return jax.ShapeDtypeStruct(shape, dtype)


def gather_parts(part):
    spread = jnp.broadcast_to(part, (lax.axis_size("feeder"),) + part.shape)
    return lax.all_to_all(spread, "feeder", 0, 0)


def local(anchor, cost_lin, dual, target, leaf_weight, q_mat, diag_gain, block_mask, ancestor):
    leaves, sections, nodes = anchor.shape
    rows = leaves * sections
    groups = lax.axis_size("scen")
    total_nodes = lax.axis_size("feeder") * nodes
    flat = lambda a: a.reshape(rows, nodes)
    sums_shape = shaped((rows // LANES, LANES))
    full, thin, slab = shaped((rows, nodes)), shaped((rows, LANES)), shaped((sections, LANES))

    sums = call(sum_kernel, (flat(anchor),), sums_shape, name="start_sums")
    got = gather_parts(sums)
    target_rows = target.reshape(rows // LANES, LANES)
    first_leaf = (lax.axis_index("scen") * leaves).astype(jnp.int32).reshape(1)
    anc = jnp.broadcast_to(ancestor.T.reshape(rows, 1), (rows, LANES))
    q_eff, fixed, z, gain, same, recip, pick, cont, scalars = call(
        prep_kernel,
        (first_leaf, leaf_weight, block_mask[0], flat(anchor), flat(cost_lin), flat(dual), q_mat,
         diag_gain.reshape(1, nodes), anc),
        (shaped((nodes, nodes), jnp.bfloat16), full, full, shaped((1, nodes)), thin, thin, thin,
         slab, slab),
        in_specs=[SMEM] * 3 + [VMEM] * 6,
        name="prep",
    )
    for sweep in range(PROX_ITERS - 1):
        sums, z = call(
            lambda *refs: step_kernel(total_nodes, *refs),
            (got, target_rows, z, q_eff, fixed, gain),
            (sums_shape, full),
            scratch=(pltpu.VMEM((rows, nodes), jnp.float32),),
            name="prox_step",
        )
        got = gather_parts(sums)
    x, own, sent = call(
        lambda *refs: last_kernel(total_nodes, *refs),
        (leaf_weight, got, target_rows, z, same, recip, cont, scalars),
        (full, full, shaped((groups, 24, LANES))),
        in_specs=[SMEM] + [VMEM] * 7,
        scratch=(pltpu.VMEM((sections, nodes), jnp.float32),) * 2,
        name="last_step",
    )
    got = lax.all_to_all(sent, "scen", 0, 0)
    back = call(owner_kernel, (got,), shaped((groups, 16, LANES)), name="owner_chain")
    got = lax.all_to_all(back, "scen", 0, 0)
    average, new_dual = call(
        final_kernel,
        (got, own, pick, x, flat(dual)),
        (full, full),
        out_specs=(HBM, HBM),
        scratch=(
            (pltpu.VMEM((sections, nodes), jnp.float32),) * 2
            + (pltpu.VMEM((rows, nodes), jnp.float32),) * 2
            + (pltpu.SemaphoreType.DMA((2, 4)),)
        ),
        name="finish",
    )
    whole = lambda a: a.reshape(leaves, sections, nodes)
    return (whole(x), whole(average), whole(new_dual))


def solution(mesh):
    return jax.shard_map(
        local,
        mesh=mesh,
        in_specs=(
            P("scen", None, "feeder"),
            P("scen", None, "feeder"),
            P("scen", None, "feeder"),
            P("scen", None),
            P("scen"),
            P("feeder", None),
            P("feeder"),
            P("feeder", None, None),
            P(None, "scen"),
        ),
        out_specs=(P("scen", None, "feeder"), P("scen", None, "feeder"), P("scen", None, "feeder")),
        check_vma=False,
    )
```

```python
import jax
import jax.numpy as jnp
from jax import lax
from jax.experimental import pallas as pl
from jax.experimental.pallas import tpu as pltpu
from jax.sharding import PartitionSpec as P

PROX_ITERS = 8
LANES = 128


penalty = 1.0
step_size = 0.08
coupling = 4.0
power_limit = 2.0

VMEM = pl.BlockSpec(memory_space=pltpu.VMEM)
SMEM = pl.BlockSpec(memory_space=pltpu.SMEM)
HBM = pl.BlockSpec(memory_space=pltpu.HBM)
PARAMS = pltpu.CompilerParams(vmem_limit_bytes=12 * 1024 * 1024)


def row_sums(block):
    total = block[:, :LANES]
    for start in range(LANES, block.shape[1], LANES):
        total = total + block[:, start : start + LANES]
    return jnp.sum(total.T, axis=0, keepdims=True)


def sum_kernel(anchor_hbm, sums_ref, anchor_ref, sems):
    copies = []
    for i in range(anchor_ref.shape[0] // LANES):
        part = pl.ds(i * LANES, LANES)
        copies.append(
            pltpu.make_async_copy(anchor_hbm.at[part, :], anchor_ref.at[part, :], sems.at[i])
        )
        copies[i].start()
    for i in range(anchor_ref.shape[0] // LANES):
        copies[i].wait()
        block = anchor_ref[i * LANES : (i + 1) * LANES, :].astype(jnp.float32)
        sums_ref[i : i + 1, :] = row_sums(block)


def affine(x, image, gain, fixed):
    return x * gain - (fixed + step_size * image)


def column(row):
    n = row.shape[1]
    down = lax.broadcasted_iota(jnp.int32, (n, n), 0)
    across = lax.broadcasted_iota(jnp.int32, (n, n), 1)
    spread = jnp.broadcast_to(row, (n, n))
    return jnp.sum(jnp.where(down == across, spread, 0.0), axis=1, keepdims=True)


def prep_kernel(
    first_ref, weight_ref, mask_ref, target_ref, anc_ref, diag_ref,
    anchor_hbm, cost_hbm, dual_hbm, q_hbm,
    q_out, fixed_out, z_out, gain_out, dual_out, thin_out,
    anchor_ref, cost_ref, q_ref, sems,
):
    moves = ((q_hbm, q_ref), (anchor_hbm, anchor_ref), (cost_hbm, cost_ref), (dual_hbm, dual_out))
    copies = [pltpu.make_async_copy(src, dst, sems.at[i]) for i, (src, dst) in enumerate(moves)]
    for copy in copies:
        copy.start()
    leaves, sections = anc_ref.shape
    rows_all = leaves * sections
    thin = (sections, LANES)
    first_leaf = first_ref[0].astype(jnp.float32)
    owner_of = anc_ref[...].astype(jnp.float32)
    anc = [jnp.broadcast_to(column(owner_of[i : i + 1, :]), thin) for i in range(leaves)]
    run, same = [], []
    for i in range(leaves):
        weight = jnp.full(thin, weight_ref[i], jnp.float32)
        same.append(jnp.where(anc[i] == anc[i - 1], 1.0, 0.0) if i else jnp.zeros(thin, jnp.float32))
        run.append(weight + same[i] * run[-1] if i else weight)
    for i in reversed(range(leaves - 1)):
        run[i] = jnp.where(same[i + 1] > 0.5, run[i + 1], run[i])
    for i in range(leaves):
        start = i * sections
        front = jnp.where(anc[i] < first_leaf, 1.0, 0.0)
        thin_out[start : start + sections, :] = same[i]
        thin_out[rows_all + start : rows_all + start + sections, :] = 1.0 / run[i]
        thin_out[2 * rows_all + start : 2 * rows_all + start + sections, :] = jnp.where(
            anc[i] == anc[-1], 2.0, front
        )
    cont = jnp.where(anc[0] < first_leaf, 1.0, 0.0)
    span = jnp.where(anc[-1] < first_leaf, 1.0, 0.0)
    end = 3 * rows_all
    thin_out[end : end + sections, :] = cont
    blocks = 8
    per = sections // 4
    section = lax.broadcasted_iota(jnp.int32, thin, 0)
    lane = lax.broadcasted_iota(jnp.int32, thin, 1)
    for block in range(4):
        place = section - block * per
        inside = (place >= 0) & (place < per)
        line = jnp.where(inside & (lane == place), run[-1], 0.0)
        line = jnp.where(inside & (lane == place + 8), run[0] * cont, line)
        line = jnp.where(inside & (lane == place + 16), span, line)
        spot = end + sections + block
        thin_out[spot : spot + 1, :] = jnp.sum(line, axis=0, keepdims=True)
    thin_out[end + sections + 4 : end + sections + blocks, :] = jnp.zeros((4, LANES), jnp.float32)
    gain = 1.0 - step_size * (2.0 * diag_ref[...] + penalty)
    gain_out[...] = gain

    count = mask_ref.shape[0]
    width = q_ref.shape[0] // count
    copies[0].wait()
    for i in range(count):
        for j in range(count):
            rows, cols = slice(i * width, (i + 1) * width), slice(j * width, (j + 1) * width)
            keep = mask_ref[i, j].astype(jnp.float32).astype(jnp.bfloat16)
            q_out[rows, cols] = q_ref[rows, cols] * keep
    copies[1].wait()
    image = jnp.dot(anchor_ref[...], q_out[...], preferred_element_type=jnp.float32)
    z_out[...] = image
    copies[2].wait()
    copies[3].wait()
    for i in range(leaves):
        rows = slice(i * sections, (i + 1) * sections)
        pull = (step_size * coupling) * column(target_ref[i : i + 1, :])
        start_pt = anchor_ref[rows, :].astype(jnp.float32)
        linear = cost_ref[rows, :].astype(jnp.float32) + dual_out[rows, :] - penalty * start_pt
        fixed = step_size * linear - pull
        fixed_out[rows, :] = fixed
        z_out[rows, :] = affine(start_pt, z_out[rows, :], gain, fixed)


def clipped(total_nodes, got_ref, z_ref, x_ref):
    shift = jnp.sum(got_ref[...], axis=0) * (step_size * coupling / total_nodes)
    for i in range(z_ref.shape[0] // LANES):
        rows = slice(i * LANES, (i + 1) * LANES)
        tile = jnp.broadcast_to(shift[i : i + 1, :], (LANES, LANES)).T
        for start in range(0, z_ref.shape[1], LANES):
            cols = slice(start, start + LANES)
            x_ref[rows, cols] = jnp.clip(z_ref[rows, cols] - tile, -power_limit, power_limit)


def step_kernel(
    total_nodes, got_ref, z_ref, q_ref, fixed_ref, gain_ref, sums_ref, z_out, x_ref
):
    clipped(total_nodes, got_ref, z_ref, x_ref)
    for i in range(x_ref.shape[0] // LANES):
        sums_ref[i : i + 1, :] = row_sums(x_ref[i * LANES : (i + 1) * LANES, :])
    x = x_ref[...]
    image = jnp.dot(x.astype(jnp.bfloat16), q_ref[...], preferred_element_type=jnp.float32)
    z_out[...] = affine(x, image, gain_ref[...], fixed_ref[...])


def last_kernel(
    total_nodes, weight_ref, got_ref, z_ref, thin_ref,
    x_hbm, own_ref, sent_ref,
    x_ref, tail_ref, head_ref, sem,
):
    clipped(total_nodes, got_ref, z_ref, x_ref)
    copy = pltpu.make_async_copy(x_ref, x_hbm, sem)
    copy.start()
    leaves = weight_ref.shape[0]
    rows_all, nodes = x_ref.shape
    sections = rows_all // leaves
    owners = sent_ref.shape[0]
    node_blocks = nodes // LANES
    per = sections * node_blocks // owners
    end = 3 * rows_all
    for start in range(0, nodes, LANES):
        cols = slice(start, start + LANES)
        run = []
        for i in range(leaves):
            rows = slice(i * sections, (i + 1) * sections)
            term = weight_ref[i] * x_ref[rows, cols]
            run.append(term if i == 0 else term + thin_ref[rows, :] * run[-1])
        total = run[-1]
        tail_ref[:, cols] = total
        for i in reversed(range(leaves)):
            rows = slice(i * sections, (i + 1) * sections)
            if i < leaves - 1:
                later = slice((i + 1) * sections, (i + 2) * sections)
                total = jnp.where(thin_ref[later, :] > 0.5, total, run[i])
            recip = slice(rows_all + i * sections, rows_all + (i + 1) * sections)
            own_ref[rows, cols] = total * thin_ref[recip, :]
        head_ref[:, cols] = total * thin_ref[end : end + sections, :]
    zeros = jnp.zeros((8 - per, LANES), jnp.float32)
    for owner in range(owners):
        block, col = owner // node_blocks, owner % node_blocks
        rows, cols = slice(block * per, (block + 1) * per), slice(col * LANES, (col + 1) * LANES)
        spot = end + sections + block
        sent_ref[owner, 0:per, :] = tail_ref[rows, cols]
        sent_ref[owner, per:8, :] = zeros
        sent_ref[owner, per : per + 1, :] = thin_ref[spot : spot + 1, :]
        sent_ref[owner, 8 : 8 + per, :] = head_ref[rows, cols]
        sent_ref[owner, 8 + per : 16, :] = zeros
    copy.wait()


def owner_kernel(got_ref, back_ref):
    per = back_ref.shape[1] * back_ref.shape[2] // 2
    groups = got_ref.shape[0]
    shape = (8, LANES)
    tails = [got_ref[g, 0:8, :] for g in range(groups)]
    heads = [got_ref[g, 8:16, :] for g in range(groups)]
    down = lax.broadcasted_iota(jnp.int32, shape, 0)
    across = lax.broadcasted_iota(jnp.int32, shape, 1)

    def scalars(g, first):
        line = jnp.broadcast_to(got_ref[g, per : per + 1, :], shape)
        mine = jnp.where(across == down + first, line, 0.0)
        return jnp.broadcast_to(jnp.sum(mine, axis=1, keepdims=True), shape)

    tail_w = [scalars(g, 0) for g in range(groups)]
    head_w = [scalars(g, 8) for g in range(groups)]
    spans = [scalars(g, 16) for g in range(groups)]
    zero = jnp.zeros(shape, jnp.float32)
    before, before_w, after, after_w = [zero], [zero], [zero], [zero]
    for g in range(groups - 1):
        before.append(tails[g] + spans[g] * before[-1])
        before_w.append(tail_w[g] + spans[g] * before_w[-1])
    for g in reversed(range(1, groups)):
        after.insert(0, heads[g] + spans[g] * after[0])
        after_w.insert(0, head_w[g] + spans[g] * after_w[0])
    for g in range(groups):
        first_w = before_w[g] + head_w[g] + spans[g] * after_w[g]
        last_w = tail_w[g] + after_w[g] + spans[g] * before_w[g]
        first_w = jnp.where(first_w > 0.0, first_w, 1.0)
        last_w = jnp.where(last_w > 0.0, last_w, 1.0)
        first = (before[g] + heads[g] + spans[g] * after[g]) / first_w
        last = (tails[g] + after[g] + spans[g] * before[g]) / last_w
        for i, row in enumerate((first, last)):
            for j in range(per):
                spot = i * per + j
                back_ref[g, spot // 4, spot % 4 : spot % 4 + 1, :] = row[j : j + 1]


def final_kernel(
    got_ref, own_ref, thin_ref, x_ref, dual_ref, average_hbm, new_dual_hbm,
    first_ref, last_ref, average_ref, new_dual_ref, sems,
):
    owners = got_ref.shape[0]
    sections, nodes = first_ref.shape
    node_blocks = nodes // LANES
    per = sections * node_blocks // owners
    for owner in range(owners):
        block, col = owner // node_blocks, owner % node_blocks
        cols = slice(col * LANES, (col + 1) * LANES)
        for i, edge_ref in enumerate((first_ref, last_ref)):
            for j in range(per):
                spot, row = i * per + j, block * per + j
                edge_ref[row : row + 1, cols] = got_ref[owner, spot // 4, spot % 4 : spot % 4 + 1, :]
    leaves = x_ref.shape[0] // sections
    chunks = sems.shape[1]
    each = leaves // chunks
    copies = []
    for chunk in range(chunks):
        for i in range(chunk * each, (chunk + 1) * each):
            rows = slice(i * sections, (i + 1) * sections)
            offset = 2 * leaves * sections + i * sections
            pick = thin_ref[offset : offset + sections, :]
            for start in range(0, nodes, LANES):
                cols = slice(start, start + LANES)
                ends = jnp.where(pick > 1.5, last_ref[:, cols], first_ref[:, cols])
                average = jnp.where(pick > 0.5, ends, own_ref[rows, cols])
                average_ref[rows, cols] = average
                new_dual_ref[rows, cols] = dual_ref[rows, cols] + penalty * (
                    x_ref[rows, cols] - average
                )
        part = pl.ds(chunk * each * sections, each * sections)
        for n, (src, dst) in enumerate(((average_ref, average_hbm), (new_dual_ref, new_dual_hbm))):
            copy = pltpu.make_async_copy(src.at[part, :], dst.at[part, :], sems.at[n, chunk])
            copy.start()
            copies.append(copy)
    for copy in copies:
        copy.wait()


def call(kernel, inputs, outputs, in_specs=None, out_specs=None, scratch=(), name=None):
    return pl.pallas_call(
        kernel,
        out_shape=outputs,
        in_specs=in_specs or [VMEM] * len(inputs),
        out_specs=out_specs or jax.tree.map(lambda _: VMEM, outputs),
        scratch_shapes=scratch,
        compiler_params=PARAMS,
        name=name,
    )(*inputs)


def shaped(shape, dtype=jnp.float32):
    return jax.ShapeDtypeStruct(shape, dtype)


def gather_parts(part):
    spread = jnp.broadcast_to(part, (lax.axis_size("feeder"),) + part.shape)
    return lax.all_to_all(spread, "feeder", 0, 0)


def local(anchor, cost_lin, dual, target, leaf_weight, q_mat, diag_gain, block_mask, ancestor):
    leaves, sections, nodes = anchor.shape
    rows = leaves * sections
    groups = lax.axis_size("scen")
    total_nodes = lax.axis_size("feeder") * nodes
    flat = lambda a: a.reshape(rows, nodes)
    sums_shape = shaped((rows // LANES, LANES))
    full, small = shaped((rows, nodes)), shaped((3 * rows + sections + 8, LANES))
    buffer = pltpu.VMEM((rows, nodes), jnp.float32)
    edge = pltpu.VMEM((sections, nodes), jnp.float32)

    sums = call(
        sum_kernel,
        (flat(anchor),),
        sums_shape,
        in_specs=[HBM],
        scratch=(pltpu.VMEM((rows, nodes), jnp.bfloat16), pltpu.SemaphoreType.DMA((rows // LANES,))),
        name="start_sums",
    )
    got = gather_parts(sums)
    first_leaf = (lax.axis_index("scen") * leaves).astype(jnp.int32).reshape(1)
    q_eff, fixed, z, gain, dual_near, thin = call(
        prep_kernel,
        (first_leaf, leaf_weight, block_mask[0], target, ancestor.T, diag_gain.reshape(1, nodes),
         flat(anchor), flat(cost_lin), flat(dual), q_mat),
        (shaped((nodes, nodes), jnp.bfloat16), full, full, shaped((1, nodes)), full, small),
        in_specs=[SMEM] * 3 + [VMEM] * 3 + [HBM] * 4,
        scratch=(
            pltpu.VMEM((rows, nodes), jnp.bfloat16),
            pltpu.VMEM((rows, nodes), jnp.bfloat16),
            pltpu.VMEM((nodes, nodes), jnp.bfloat16),
            pltpu.SemaphoreType.DMA((4,)),
        ),
        name="prep",
    )
    for sweep in range(PROX_ITERS - 1):
        sums, z = call(
            lambda *refs: step_kernel(total_nodes, *refs),
            (got, z, q_eff, fixed, gain),
            (sums_shape, full),
            scratch=(buffer,),
            name="prox_step",
        )
        got = gather_parts(sums)
    x, own, sent = call(
        lambda *refs: last_kernel(total_nodes, *refs),
        (leaf_weight, got, z, thin),
        (full, full, shaped((groups, 16, LANES))),
        in_specs=[SMEM] + [VMEM] * 3,
        out_specs=(HBM, VMEM, VMEM),
        scratch=(buffer, edge, edge, pltpu.SemaphoreType.DMA),
        name="last_step",
    )
    per = sections * (nodes // LANES) // groups
    got = lax.all_to_all(sent, "scen", 0, 0)
    back = call(owner_kernel, (got,), shaped((groups, per // 2, 4, LANES)), name="owner_chain")
    got = lax.all_to_all(back, "scen", 0, 0)
    average, new_dual = call(
        final_kernel,
        (got, own, thin, x, dual_near),
        (full, full),
        out_specs=(HBM, HBM),
        scratch=(edge, edge, buffer, buffer, pltpu.SemaphoreType.DMA((2, 4))),
        name="finish",
    )
    whole = lambda a: a.reshape(leaves, sections, nodes)
    return (whole(x), whole(average), whole(new_dual))


def solution(mesh):
    return jax.shard_map(
        local,
        mesh=mesh,
        in_specs=(
            P("scen", None, "feeder"),
            P("scen", None, "feeder"),
            P("scen", None, "feeder"),
            P("scen", None),
            P("scen"),
            P("feeder", None),
            P("feeder"),
            P("feeder", None, None),
            P(None, "scen"),
        ),
        out_specs=(P("scen", None, "feeder"), P("scen", None, "feeder"), P("scen", None, "feeder")),
        check_vma=False,
    )
```

```python
import jax
import jax.numpy as jnp
from jax import lax
from jax.experimental import pallas as pl
from jax.experimental.pallas import tpu as pltpu
from jax.sharding import PartitionSpec as P

PROX_ITERS = 8
LANES = 128


penalty = 1.0
step_size = 0.08
coupling = 4.0
power_limit = 2.0

VMEM = pl.BlockSpec(memory_space=pltpu.VMEM)
SMEM = pl.BlockSpec(memory_space=pltpu.SMEM)
HBM = pl.BlockSpec(memory_space=pltpu.HBM)
PARAMS = pltpu.CompilerParams(vmem_limit_bytes=12 * 1024 * 1024)
PREP_PARAMS = pltpu.CompilerParams()


def row_sums(block):
    total = block[:, :LANES]
    for start in range(LANES, block.shape[1], LANES):
        total = total + block[:, start : start + LANES]
    return jnp.sum(total.T, axis=0, keepdims=True)


def affine(x, image, gain, fixed):
    return x * gain - (fixed + step_size * image)


def column(row):
    n = row.shape[1]
    down = lax.broadcasted_iota(jnp.int32, (n, n), 0)
    across = lax.broadcasted_iota(jnp.int32, (n, n), 1)
    spread = jnp.broadcast_to(row, (n, n))
    return jnp.sum(jnp.where(down == across, spread, 0.0), axis=1, keepdims=True)


def prep_kernel(
    first_ref, weight_ref, mask_ref, target_ref, anc_ref, diag_ref,
    anchor_hbm, cost_hbm, dual_hbm, q_hbm,
    sums_ref, q_out, fixed_out, z_out, gain_out, thin_out,
    anchor_ref, cost_ref, dual_ref, q_ref, sems,
):
    moves = ((anchor_hbm, anchor_ref), (q_hbm, q_ref), (cost_hbm, cost_ref), (dual_hbm, dual_ref))
    copies = [pltpu.make_async_copy(src, dst, sems.at[i]) for i, (src, dst) in enumerate(moves)]
    for copy in copies:
        copy.start()
    leaves, sections = anc_ref.shape
    rows_all = leaves * sections
    thin = (sections, LANES)
    first_leaf = first_ref[0].astype(jnp.float32)
    owner_of = anc_ref[...].astype(jnp.float32)
    anc = [jnp.broadcast_to(column(owner_of[i : i + 1, :]), thin) for i in range(leaves)]
    run, same = [], []
    for i in range(leaves):
        weight = jnp.full(thin, weight_ref[i], jnp.float32)
        same.append(jnp.where(anc[i] == anc[i - 1], 1.0, 0.0) if i else jnp.zeros(thin, jnp.float32))
        run.append(weight + same[i] * run[-1] if i else weight)
    for i in reversed(range(leaves - 1)):
        run[i] = jnp.where(same[i + 1] > 0.5, run[i + 1], run[i])
    for i in range(leaves):
        start = i * sections
        front = jnp.where(anc[i] < first_leaf, 1.0, 0.0)
        thin_out[start : start + sections, :] = same[i]
        thin_out[rows_all + start : rows_all + start + sections, :] = 1.0 / run[i]
        thin_out[2 * rows_all + start : 2 * rows_all + start + sections, :] = jnp.where(
            anc[i] == anc[-1], 2.0, front
        )
    cont = jnp.where(anc[0] < first_leaf, 1.0, 0.0)
    span = jnp.where(anc[-1] < first_leaf, 1.0, 0.0)
    end = 3 * rows_all
    thin_out[end : end + sections, :] = cont
    blocks = 8
    per = sections // 4
    section = lax.broadcasted_iota(jnp.int32, thin, 0)
    lane = lax.broadcasted_iota(jnp.int32, thin, 1)
    for block in range(4):
        place = section - block * per
        inside = (place >= 0) & (place < per)
        line = jnp.where(inside & (lane == place), run[-1], 0.0)
        line = jnp.where(inside & (lane == place + 8), run[0] * cont, line)
        line = jnp.where(inside & (lane == place + 16), span, line)
        spot = end + sections + block
        thin_out[spot : spot + 1, :] = jnp.sum(line, axis=0, keepdims=True)
    thin_out[end + sections + 4 : end + sections + blocks, :] = jnp.zeros((4, LANES), jnp.float32)
    gain = 1.0 - step_size * (2.0 * diag_ref[...] + penalty)
    gain_out[...] = gain

    count = mask_ref.shape[0]
    width = q_ref.shape[0] // count
    copies[0].wait()
    for i in range(rows_all // LANES):
        block = anchor_ref[i * LANES : (i + 1) * LANES, :].astype(jnp.float32)
        sums_ref[i : i + 1, :] = row_sums(block)
    copies[1].wait()
    for i in range(count):
        for j in range(count):
            rows, cols = slice(i * width, (i + 1) * width), slice(j * width, (j + 1) * width)
            keep = mask_ref[i, j].astype(jnp.float32).astype(jnp.bfloat16)
            q_out[rows, cols] = q_ref[rows, cols] * keep
    image = jnp.dot(anchor_ref[...], q_out[...], preferred_element_type=jnp.float32)
    z_out[...] = image
    copies[2].wait()
    copies[3].wait()
    for i in range(leaves):
        rows = slice(i * sections, (i + 1) * sections)
        pull = (step_size * coupling) * column(target_ref[i : i + 1, :])
        start_pt = anchor_ref[rows, :].astype(jnp.float32)
        linear = cost_ref[rows, :].astype(jnp.float32) + dual_ref[rows, :] - penalty * start_pt
        fixed = step_size * linear - pull
        fixed_out[rows, :] = fixed
        z_out[rows, :] = affine(start_pt, z_out[rows, :], gain, fixed)


def clipped(total_nodes, got_ref, z_ref, x_ref):
    shift = jnp.sum(got_ref[...], axis=0) * (step_size * coupling / total_nodes)
    for i in range(z_ref.shape[0] // LANES):
        rows = slice(i * LANES, (i + 1) * LANES)
        tile = jnp.broadcast_to(shift[i : i + 1, :], (LANES, LANES)).T
        for start in range(0, z_ref.shape[1], LANES):
            cols = slice(start, start + LANES)
            x_ref[rows, cols] = jnp.clip(z_ref[rows, cols] - tile, -power_limit, power_limit)


def step_kernel(
    total_nodes, got_ref, z_ref, q_ref, fixed_ref, gain_ref, sums_ref, z_out, x_ref
):
    clipped(total_nodes, got_ref, z_ref, x_ref)
    for i in range(x_ref.shape[0] // LANES):
        sums_ref[i : i + 1, :] = row_sums(x_ref[i * LANES : (i + 1) * LANES, :])
    x = x_ref[...]
    image = jnp.dot(x.astype(jnp.bfloat16), q_ref[...], preferred_element_type=jnp.float32)
    z_out[...] = affine(x, image, gain_ref[...], fixed_ref[...])


def last_kernel(
    total_nodes, weight_ref, got_ref, z_ref, thin_ref,
    x_ref, own_ref, sent_ref, tail_ref, head_ref,
):
    clipped(total_nodes, got_ref, z_ref, x_ref)
    leaves = weight_ref.shape[0]
    rows_all, nodes = x_ref.shape
    sections = rows_all // leaves
    owners = sent_ref.shape[0]
    node_blocks = nodes // LANES
    per = sections * node_blocks // owners
    end = 3 * rows_all
    for start in range(0, nodes, LANES):
        cols = slice(start, start + LANES)
        run = []
        for i in range(leaves):
            rows = slice(i * sections, (i + 1) * sections)
            term = weight_ref[i] * x_ref[rows, cols]
            run.append(term if i == 0 else term + thin_ref[rows, :] * run[-1])
        total = run[-1]
        tail_ref[:, cols] = total
        for i in reversed(range(leaves)):
            rows = slice(i * sections, (i + 1) * sections)
            if i < leaves - 1:
                later = slice((i + 1) * sections, (i + 2) * sections)
                total = jnp.where(thin_ref[later, :] > 0.5, total, run[i])
            recip = slice(rows_all + i * sections, rows_all + (i + 1) * sections)
            own_ref[rows, cols] = total * thin_ref[recip, :]
        head_ref[:, cols] = total * thin_ref[end : end + sections, :]
    zeros = jnp.zeros((8 - per, LANES), jnp.float32)
    for owner in range(owners):
        block, col = owner // node_blocks, owner % node_blocks
        rows, cols = slice(block * per, (block + 1) * per), slice(col * LANES, (col + 1) * LANES)
        spot = end + sections + block
        sent_ref[owner, 0:per, :] = tail_ref[rows, cols]
        sent_ref[owner, per:8, :] = zeros
        sent_ref[owner, per : per + 1, :] = thin_ref[spot : spot + 1, :]
        sent_ref[owner, 8 : 8 + per, :] = head_ref[rows, cols]
        sent_ref[owner, 8 + per : 16, :] = zeros


def owner_kernel(got_ref, back_ref):
    per = back_ref.shape[1] * back_ref.shape[2] // 2
    groups = got_ref.shape[0]
    shape = (8, LANES)
    tails = [got_ref[g, 0:8, :] for g in range(groups)]
    heads = [got_ref[g, 8:16, :] for g in range(groups)]
    down = lax.broadcasted_iota(jnp.int32, shape, 0)
    across = lax.broadcasted_iota(jnp.int32, shape, 1)

    def scalars(g, first):
        line = jnp.broadcast_to(got_ref[g, per : per + 1, :], shape)
        mine = jnp.where(across == down + first, line, 0.0)
        return jnp.broadcast_to(jnp.sum(mine, axis=1, keepdims=True), shape)

    tail_w = [scalars(g, 0) for g in range(groups)]
    head_w = [scalars(g, 8) for g in range(groups)]
    spans = [scalars(g, 16) for g in range(groups)]
    zero = jnp.zeros(shape, jnp.float32)
    before, before_w, after, after_w = [zero], [zero], [zero], [zero]
    for g in range(groups - 1):
        before.append(tails[g] + spans[g] * before[-1])
        before_w.append(tail_w[g] + spans[g] * before_w[-1])
    for g in reversed(range(1, groups)):
        after.insert(0, heads[g] + spans[g] * after[0])
        after_w.insert(0, head_w[g] + spans[g] * after_w[0])
    for g in range(groups):
        first_w = before_w[g] + head_w[g] + spans[g] * after_w[g]
        last_w = tail_w[g] + after_w[g] + spans[g] * before_w[g]
        first_w = jnp.where(first_w > 0.0, first_w, 1.0)
        last_w = jnp.where(last_w > 0.0, last_w, 1.0)
        first = (before[g] + heads[g] + spans[g] * after[g]) / first_w
        last = (tails[g] + after[g] + spans[g] * before[g]) / last_w
        for i, row in enumerate((first, last)):
            for j in range(per):
                spot = i * per + j
                back_ref[g, spot // 4, spot % 4 : spot % 4 + 1, :] = row[j : j + 1]


def final_kernel(
    got_ref, own_ref, thin_ref, x_ref, dual_ref, x_hbm, average_hbm, new_dual_hbm,
    first_ref, last_ref, average_ref, new_dual_ref, sems, x_sem,
):
    copies = [pltpu.make_async_copy(x_ref, x_hbm, x_sem)]
    copies[0].start()
    owners = got_ref.shape[0]
    sections, nodes = first_ref.shape
    node_blocks = nodes // LANES
    per = sections * node_blocks // owners
    for owner in range(owners):
        block, col = owner // node_blocks, owner % node_blocks
        cols = slice(col * LANES, (col + 1) * LANES)
        for i, edge_ref in enumerate((first_ref, last_ref)):
            for j in range(per):
                spot, row = i * per + j, block * per + j
                edge_ref[row : row + 1, cols] = got_ref[owner, spot // 4, spot % 4 : spot % 4 + 1, :]
    leaves = x_ref.shape[0] // sections
    chunks = sems.shape[1]
    each = leaves // chunks
    for chunk in range(chunks):
        for i in range(chunk * each, (chunk + 1) * each):
            rows = slice(i * sections, (i + 1) * sections)
            offset = 2 * leaves * sections + i * sections
            pick = thin_ref[offset : offset + sections, :]
            for start in range(0, nodes, LANES):
                cols = slice(start, start + LANES)
                ends = jnp.where(pick > 1.5, last_ref[:, cols], first_ref[:, cols])
                average = jnp.where(pick > 0.5, ends, own_ref[rows, cols])
                average_ref[rows, cols] = average
                new_dual_ref[rows, cols] = dual_ref[rows, cols] + penalty * (
                    x_ref[rows, cols] - average
                )
        part = pl.ds(chunk * each * sections, each * sections)
        for n, (src, dst) in enumerate(((average_ref, average_hbm), (new_dual_ref, new_dual_hbm))):
            copy = pltpu.make_async_copy(src.at[part, :], dst.at[part, :], sems.at[n, chunk])
            copy.start()
            copies.append(copy)
    for copy in copies:
        copy.wait()


def call(kernel, inputs, outputs, in_specs=None, out_specs=None, scratch=(), params=PARAMS, name=None):
    return pl.pallas_call(
        kernel,
        out_shape=outputs,
        in_specs=in_specs or [VMEM] * len(inputs),
        out_specs=out_specs or jax.tree.map(lambda _: VMEM, outputs),
        scratch_shapes=scratch,
        compiler_params=params,
        name=name,
    )(*inputs)


def shaped(shape, dtype=jnp.float32):
    return jax.ShapeDtypeStruct(shape, dtype)


def gather_parts(part):
    spread = jnp.broadcast_to(part, (lax.axis_size("feeder"),) + part.shape)
    return lax.all_to_all(spread, "feeder", 0, 0)


def local(anchor, cost_lin, dual, target, leaf_weight, q_mat, diag_gain, block_mask, ancestor):
    leaves, sections, nodes = anchor.shape
    rows = leaves * sections
    groups = lax.axis_size("scen")
    total_nodes = lax.axis_size("feeder") * nodes
    flat = lambda a: a.reshape(rows, nodes)
    sums_shape = shaped((rows // LANES, LANES))
    full, small = shaped((rows, nodes)), shaped((3 * rows + sections + 8, LANES))
    buffer = pltpu.VMEM((rows, nodes), jnp.float32)
    edge = pltpu.VMEM((sections, nodes), jnp.float32)

    first_leaf = (lax.axis_index("scen") * leaves).astype(jnp.int32).reshape(1)
    narrow = pltpu.VMEM((rows, nodes), jnp.bfloat16)
    sums, q_eff, fixed, z, gain, thin = call(
        prep_kernel,
        (first_leaf, leaf_weight, block_mask[0], target, ancestor.T, diag_gain.reshape(1, nodes),
         flat(anchor), flat(cost_lin), flat(dual), q_mat),
        (sums_shape, shaped((nodes, nodes), jnp.bfloat16), full, full, shaped((1, nodes)), small),
        in_specs=[SMEM] * 3 + [VMEM] * 3 + [HBM] * 4,
        scratch=(
            narrow, narrow, buffer, pltpu.VMEM((nodes, nodes), jnp.bfloat16),
            pltpu.SemaphoreType.DMA((4,)),
        ),
        params=PREP_PARAMS,
        name="prep",
    )
    got = gather_parts(sums)
    for sweep in range(PROX_ITERS - 1):
        sums, z = call(
            lambda *refs: step_kernel(total_nodes, *refs),
            (got, z, q_eff, fixed, gain),
            (sums_shape, full),
            scratch=(buffer,),
            name="prox_step",
        )
        got = gather_parts(sums)
    x, own, sent = call(
        lambda *refs: last_kernel(total_nodes, *refs),
        (leaf_weight, got, z, thin),
        (full, full, shaped((groups, 16, LANES))),
        in_specs=[SMEM] + [VMEM] * 3,
        scratch=(edge, edge),
        name="last_step",
    )
    per = sections * (nodes // LANES) // groups
    got = lax.all_to_all(sent, "scen", 0, 0)
    back = call(owner_kernel, (got,), shaped((groups, per // 2, 4, LANES)), name="owner_chain")
    got = lax.all_to_all(back, "scen", 0, 0)
    x, average, new_dual = call(
        final_kernel,
        (got, own, thin, x, flat(dual)),
        (full, full, full),
        out_specs=(HBM, HBM, HBM),
        scratch=(
            edge, edge, buffer, buffer, pltpu.SemaphoreType.DMA((2, 4)), pltpu.SemaphoreType.DMA
        ),
        name="finish",
    )
    whole = lambda a: a.reshape(leaves, sections, nodes)
    return (whole(x), whole(average), whole(new_dual))


def solution(mesh):
    return jax.shard_map(
        local,
        mesh=mesh,
        in_specs=(
            P("scen", None, "feeder"),
            P("scen", None, "feeder"),
            P("scen", None, "feeder"),
            P("scen", None),
            P("scen"),
            P("feeder", None),
            P("feeder"),
            P("feeder", None, None),
            P(None, "scen"),
        ),
        out_specs=(P("scen", None, "feeder"), P("scen", None, "feeder"), P("scen", None, "feeder")),
        check_vma=False,
    )
```

```python
import jax
import jax.numpy as jnp
from jax import lax
from jax.experimental import pallas as pl
from jax.experimental.pallas import tpu as pltpu
from jax.sharding import PartitionSpec as P

PROX_ITERS = 8
LANES = 128


penalty = 1.0
step_size = 0.08
coupling = 4.0
power_limit = 2.0

VMEM = pl.BlockSpec(memory_space=pltpu.VMEM)
SMEM = pl.BlockSpec(memory_space=pltpu.SMEM)
HBM = pl.BlockSpec(memory_space=pltpu.HBM)
PARAMS = pltpu.CompilerParams(vmem_limit_bytes=12 * 1024 * 1024)


def row_sums(block):
    total = block[:, :LANES]
    for start in range(LANES, block.shape[1], LANES):
        total = total + block[:, start : start + LANES]
    return jnp.sum(total.T, axis=0, keepdims=True)


def fetch(pairs, sems):
    copies = [pltpu.make_async_copy(src, dst, sems.at[i]) for i, (src, dst) in enumerate(pairs)]
    for copy in copies:
        copy.start()
    return copies


def sum_kernel(anchor_hbm, spread_ref, anchor_ref, sems):
    parts = [pl.ds(i * LANES, LANES) for i in range(anchor_ref.shape[0] // LANES)]
    copies = fetch([(anchor_hbm.at[part, :], anchor_ref.at[part, :]) for part in parts], sems)
    for i, part in enumerate(parts):
        copies[i].wait()
        total = row_sums(anchor_ref[part, :].astype(jnp.float32))
        for feeder in range(spread_ref.shape[0]):
            spread_ref[feeder, i : i + 1, :] = total


def affine(x, image, gain, fixed):
    return x * gain - (fixed + step_size * image)


def column(row):
    n = row.shape[1]
    down = lax.broadcasted_iota(jnp.int32, (n, n), 0)
    across = lax.broadcasted_iota(jnp.int32, (n, n), 1)
    spread = jnp.broadcast_to(row, (n, n))
    return jnp.sum(jnp.where(down == across, spread, 0.0), axis=1, keepdims=True)


def prep_kernel(
    first_ref, target_hbm, anc_hbm, weight_hbm, mask_hbm, diag_hbm,
    q_hbm, anchor_hbm, cost_hbm, dual_hbm,
    q_out, fixed_out, z_out, gain_out, thin_out,
    target_ref, anc_ref, weight_ref, mask_ref, diag_ref,
    q_ref, anchor_ref, cost_ref, dual_ref, sems,
):
    sources = (
        anc_hbm, weight_hbm, mask_hbm, diag_hbm, target_hbm, q_hbm, anchor_hbm, cost_hbm, dual_hbm
    )
    places = (
        anc_ref, weight_ref, mask_ref, diag_ref, target_ref, q_ref, anchor_ref, cost_ref, dual_ref
    )
    copies = fetch(list(zip(sources, places)), sems)
    copies[0].wait()
    copies[1].wait()
    leaves, sections = anc_ref.shape
    rows_all = leaves * sections
    thin = (sections, LANES)
    first_leaf = first_ref[0].astype(jnp.float32)
    owner_of = anc_ref[...].astype(jnp.float32)
    anc = [jnp.broadcast_to(column(owner_of[i : i + 1, :]), thin) for i in range(leaves)]
    run, same = [], []
    for i in range(leaves):
        weight = jnp.broadcast_to(weight_ref[:, i : i + 1], thin)
        thin_out[3 * rows_all + i * sections : 3 * rows_all + (i + 1) * sections, :] = weight
        same.append(jnp.where(anc[i] == anc[i - 1], 1.0, 0.0) if i else jnp.zeros(thin, jnp.float32))
        run.append(weight + same[i] * run[-1] if i else weight)
    for i in reversed(range(leaves - 1)):
        run[i] = jnp.where(same[i + 1] > 0.5, run[i + 1], run[i])
    for i in range(leaves):
        start = i * sections
        front = jnp.where(anc[i] < first_leaf, 1.0, 0.0)
        thin_out[start : start + sections, :] = same[i]
        thin_out[rows_all + start : rows_all + start + sections, :] = 1.0 / run[i]
        thin_out[2 * rows_all + start : 2 * rows_all + start + sections, :] = jnp.where(
            anc[i] == anc[-1], 2.0, front
        )
    cont = jnp.where(anc[0] < first_leaf, 1.0, 0.0)
    span = jnp.where(anc[-1] < first_leaf, 1.0, 0.0)
    end = 4 * rows_all
    thin_out[end : end + sections, :] = cont
    blocks = 8
    per = sections // 4
    section = lax.broadcasted_iota(jnp.int32, thin, 0)
    lane = lax.broadcasted_iota(jnp.int32, thin, 1)
    for block in range(4):
        place = section - block * per
        inside = (place >= 0) & (place < per)
        line = jnp.where(inside & (lane == place), run[-1], 0.0)
        line = jnp.where(inside & (lane == place + 8), run[0] * cont, line)
        line = jnp.where(inside & (lane == place + 16), span, line)
        spot = end + sections + block
        thin_out[spot : spot + 1, :] = jnp.sum(line, axis=0, keepdims=True)
    thin_out[end + sections + 4 : end + sections + blocks, :] = jnp.zeros((4, LANES), jnp.float32)
    copies[2].wait()
    copies[3].wait()
    copies[4].wait()
    gain = 1.0 - step_size * (2.0 * diag_ref[...] + penalty)
    gain_out[...] = gain

    count = mask_ref.shape[0]
    width = q_ref.shape[0] // count
    keep = mask_ref[...].astype(jnp.float32)
    copies[5].wait()
    for i in range(count):
        for j in range(count):
            rows, cols = slice(i * width, (i + 1) * width), slice(j * width, (j + 1) * width)
            block = jnp.broadcast_to(keep[i : i + 1, j : j + 1], (width, width))
            q_out[rows, cols] = q_ref[rows, cols] * block.astype(jnp.bfloat16)
    copies[6].wait()
    image = jnp.dot(anchor_ref[...], q_out[...], preferred_element_type=jnp.float32)
    z_out[...] = image
    copies[7].wait()
    copies[8].wait()
    for i in range(leaves):
        rows = slice(i * sections, (i + 1) * sections)
        pull = (step_size * coupling) * column(target_ref[i : i + 1, :])
        start_pt = anchor_ref[rows, :].astype(jnp.float32)
        linear = cost_ref[rows, :].astype(jnp.float32) + dual_ref[rows, :] - penalty * start_pt
        fixed = step_size * linear - pull
        fixed_out[rows, :] = fixed
        z_out[rows, :] = affine(start_pt, z_out[rows, :], gain, fixed)


def clipped(total_nodes, got_ref, z_ref, x_ref):
    shift = jnp.sum(got_ref[...], axis=0) * (step_size * coupling / total_nodes)
    for i in range(z_ref.shape[0] // LANES):
        rows = slice(i * LANES, (i + 1) * LANES)
        tile = jnp.broadcast_to(shift[i : i + 1, :], (LANES, LANES)).T
        for start in range(0, z_ref.shape[1], LANES):
            cols = slice(start, start + LANES)
            x_ref[rows, cols] = jnp.clip(z_ref[rows, cols] - tile, -power_limit, power_limit)


def step_kernel(
    total_nodes, got_ref, z_ref, q_ref, fixed_ref, gain_ref, sums_ref, z_out, x_ref
):
    clipped(total_nodes, got_ref, z_ref, x_ref)
    for i in range(x_ref.shape[0] // LANES):
        sums_ref[i : i + 1, :] = row_sums(x_ref[i * LANES : (i + 1) * LANES, :])
    x = x_ref[...]
    image = jnp.dot(x.astype(jnp.bfloat16), q_ref[...], preferred_element_type=jnp.float32)
    z_out[...] = affine(x, image, gain_ref[...], fixed_ref[...])


def last_kernel(
    total_nodes, leaves, got_ref, z_ref, thin_ref,
    x_ref, own_ref, sent_ref, tail_ref, head_ref,
):
    clipped(total_nodes, got_ref, z_ref, x_ref)
    rows_all, nodes = x_ref.shape
    sections = rows_all // leaves
    owners = sent_ref.shape[0]
    node_blocks = nodes // LANES
    per = sections * node_blocks // owners
    end = 4 * rows_all
    for start in range(0, nodes, LANES):
        cols = slice(start, start + LANES)
        run = []
        for i in range(leaves):
            rows = slice(i * sections, (i + 1) * sections)
            mine = slice(3 * rows_all + i * sections, 3 * rows_all + (i + 1) * sections)
            term = thin_ref[mine, :] * x_ref[rows, cols]
            run.append(term if i == 0 else term + thin_ref[rows, :] * run[-1])
        total = run[-1]
        tail_ref[:, cols] = total
        for i in reversed(range(leaves)):
            rows = slice(i * sections, (i + 1) * sections)
            if i < leaves - 1:
                later = slice((i + 1) * sections, (i + 2) * sections)
                total = jnp.where(thin_ref[later, :] > 0.5, total, run[i])
            recip = slice(rows_all + i * sections, rows_all + (i + 1) * sections)
            own_ref[rows, cols] = total * thin_ref[recip, :]
        head_ref[:, cols] = total * thin_ref[end : end + sections, :]
    zeros = jnp.zeros((8 - per, LANES), jnp.float32)
    for owner in range(owners):
        block, col = owner // node_blocks, owner % node_blocks
        rows, cols = slice(block * per, (block + 1) * per), slice(col * LANES, (col + 1) * LANES)
        spot = end + sections + block
        sent_ref[owner, 0:per, :] = tail_ref[rows, cols]
        sent_ref[owner, per:8, :] = zeros
        sent_ref[owner, per : per + 1, :] = thin_ref[spot : spot + 1, :]
        sent_ref[owner, 8 : 8 + per, :] = head_ref[rows, cols]
        sent_ref[owner, 8 + per : 16, :] = zeros


def owner_kernel(got_ref, back_ref):
    per = back_ref.shape[1] * back_ref.shape[2] // 2
    groups = got_ref.shape[0]
    shape = (8, LANES)
    tails = [got_ref[g, 0:8, :] for g in range(groups)]
    heads = [got_ref[g, 8:16, :] for g in range(groups)]
    down = lax.broadcasted_iota(jnp.int32, shape, 0)
    across = lax.broadcasted_iota(jnp.int32, shape, 1)

    def scalars(g, first):
        line = jnp.broadcast_to(got_ref[g, per : per + 1, :], shape)
        mine = jnp.where(across == down + first, line, 0.0)
        return jnp.broadcast_to(jnp.sum(mine, axis=1, keepdims=True), shape)

    tail_w = [scalars(g, 0) for g in range(groups)]
    head_w = [scalars(g, 8) for g in range(groups)]
    spans = [scalars(g, 16) for g in range(groups)]
    zero = jnp.zeros(shape, jnp.float32)
    before, before_w, after, after_w = [zero], [zero], [zero], [zero]
    for g in range(groups - 1):
        before.append(tails[g] + spans[g] * before[-1])
        before_w.append(tail_w[g] + spans[g] * before_w[-1])
    for g in reversed(range(1, groups)):
        after.insert(0, heads[g] + spans[g] * after[0])
        after_w.insert(0, head_w[g] + spans[g] * after_w[0])
    for g in range(groups):
        first_w = before_w[g] + head_w[g] + spans[g] * after_w[g]
        last_w = tail_w[g] + after_w[g] + spans[g] * before_w[g]
        first_w = jnp.where(first_w > 0.0, first_w, 1.0)
        last_w = jnp.where(last_w > 0.0, last_w, 1.0)
        first = (before[g] + heads[g] + spans[g] * after[g]) / first_w
        last = (tails[g] + after[g] + spans[g] * before[g]) / last_w
        for i, row in enumerate((first, last)):
            for j in range(per):
                spot = i * per + j
                back_ref[g, spot // 4, spot % 4 : spot % 4 + 1, :] = row[j : j + 1]


def final_kernel(
    got_ref, own_ref, thin_ref, x_ref, dual_ref, x_hbm, average_hbm, new_dual_hbm,
    first_ref, last_ref, average_ref, new_dual_ref, sems, x_sem,
):
    copies = [pltpu.make_async_copy(x_ref, x_hbm, x_sem)]
    copies[0].start()
    owners = got_ref.shape[0]
    sections, nodes = first_ref.shape
    node_blocks = nodes // LANES
    per = sections * node_blocks // owners
    for owner in range(owners):
        block, col = owner // node_blocks, owner % node_blocks
        cols = slice(col * LANES, (col + 1) * LANES)
        for i, edge_ref in enumerate((first_ref, last_ref)):
            for j in range(per):
                spot, row = i * per + j, block * per + j
                edge_ref[row : row + 1, cols] = got_ref[owner, spot // 4, spot % 4 : spot % 4 + 1, :]
    leaves = x_ref.shape[0] // sections
    chunks = sems.shape[1]
    each = leaves // chunks
    for chunk in range(chunks):
        for i in range(chunk * each, (chunk + 1) * each):
            rows = slice(i * sections, (i + 1) * sections)
            offset = 2 * leaves * sections + i * sections
            pick = thin_ref[offset : offset + sections, :]
            for start in range(0, nodes, LANES):
                cols = slice(start, start + LANES)
                ends = jnp.where(pick > 1.5, last_ref[:, cols], first_ref[:, cols])
                average = jnp.where(pick > 0.5, ends, own_ref[rows, cols])
                average_ref[rows, cols] = average
                new_dual_ref[rows, cols] = dual_ref[rows, cols] + penalty * (
                    x_ref[rows, cols] - average
                )
        part = pl.ds(chunk * each * sections, each * sections)
        for n, (src, dst) in enumerate(((average_ref, average_hbm), (new_dual_ref, new_dual_hbm))):
            copy = pltpu.make_async_copy(src.at[part, :], dst.at[part, :], sems.at[n, chunk])
            copy.start()
            copies.append(copy)
    for copy in copies:
        copy.wait()


def call(kernel, inputs, outputs, in_specs=None, out_specs=None, scratch=(), name=None):
    return pl.pallas_call(
        kernel,
        out_shape=outputs,
        in_specs=in_specs or [VMEM] * len(inputs),
        out_specs=out_specs or jax.tree.map(lambda _: VMEM, outputs),
        scratch_shapes=scratch,
        compiler_params=PARAMS,
        name=name,
    )(*inputs)


def shaped(shape, dtype=jnp.float32):
    return jax.ShapeDtypeStruct(shape, dtype)


def far(array):
    return pltpu.with_memory_space_constraint(array, pltpu.HBM)


def gather_parts(part):
    spread = jnp.broadcast_to(part, (lax.axis_size("feeder"),) + part.shape)
    return lax.all_to_all(spread, "feeder", 0, 0)


def local(anchor, cost_lin, dual, target, leaf_weight, q_mat, diag_gain, block_mask, ancestor):
    leaves, sections, nodes = anchor.shape
    rows = leaves * sections
    groups = lax.axis_size("scen")
    total_nodes = lax.axis_size("feeder") * nodes
    flat = lambda a: a.reshape(rows, nodes)
    sums_shape = shaped((rows // LANES, LANES))
    full, small = shaped((rows, nodes)), shaped((4 * rows + sections + 8, LANES))
    buffer = pltpu.VMEM((rows, nodes), jnp.float32)
    edge = pltpu.VMEM((sections, nodes), jnp.float32)

    narrow = pltpu.VMEM((rows, nodes), jnp.bfloat16)
    spread = call(
        sum_kernel,
        (far(flat(anchor)),),
        shaped((lax.axis_size("feeder"),) + sums_shape.shape),
        in_specs=[HBM],
        scratch=(narrow, pltpu.SemaphoreType.DMA((rows // LANES,))),
        name="start_sums",
    )
    got = lax.all_to_all(spread, "feeder", 0, 0)
    first_leaf = (lax.axis_index("scen") * leaves).astype(jnp.int32).reshape(1)
    small_args = (
        target, ancestor.T, leaf_weight.reshape(1, leaves), block_mask[0],
        diag_gain.reshape(1, nodes),
    )
    large_args = (q_mat, flat(anchor), flat(cost_lin), flat(dual))
    q_eff, fixed, z, gain, thin = call(
        prep_kernel,
        (first_leaf,) + tuple(far(a) for a in small_args + large_args),
        (shaped((nodes, nodes), jnp.bfloat16), full, full, shaped((1, nodes)), small),
        in_specs=[SMEM] + [HBM] * 9,
        scratch=tuple(pltpu.VMEM(a.shape, a.dtype) for a in small_args + large_args)
        + (pltpu.SemaphoreType.DMA((9,)),),
        name="prep",
    )
    for sweep in range(PROX_ITERS - 1):
        sums, z = call(
            lambda *refs: step_kernel(total_nodes, *refs),
            (got, z, q_eff, fixed, gain),
            (sums_shape, full),
            scratch=(buffer,),
            name="prox_step",
        )
        got = gather_parts(sums)
    x, own, sent = call(
        lambda *refs: last_kernel(total_nodes, leaves, *refs),
        (got, z, thin),
        (full, full, shaped((groups, 16, LANES))),
        scratch=(edge, edge),
        name="last_step",
    )
    per = sections * (nodes // LANES) // groups
    got = lax.all_to_all(sent, "scen", 0, 0)
    back = call(owner_kernel, (got,), shaped((groups, per // 2, 4, LANES)), name="owner_chain")
    got = lax.all_to_all(back, "scen", 0, 0)
    x, average, new_dual = call(
        final_kernel,
        (got, own, thin, x, flat(dual)),
        (full, full, full),
        out_specs=(HBM, HBM, HBM),
        scratch=(
            edge, edge, buffer, buffer, pltpu.SemaphoreType.DMA((2, 4)), pltpu.SemaphoreType.DMA
        ),
        name="finish",
    )
    whole = lambda a: a.reshape(leaves, sections, nodes)
    return (whole(x), whole(average), whole(new_dual))


def solution(mesh):
    return jax.shard_map(
        local,
        mesh=mesh,
        in_specs=(
            P("scen", None, "feeder"),
            P("scen", None, "feeder"),
            P("scen", None, "feeder"),
            P("scen", None),
            P("scen"),
            P("feeder", None),
            P("feeder"),
            P("feeder", None, None),
            P(None, "scen"),
        ),
        out_specs=(P("scen", None, "feeder"), P("scen", None, "feeder"), P("scen", None, "feeder")),
        check_vma=False,
    )
```

```python
import jax
import jax.numpy as jnp
from jax import lax
from jax.experimental import pallas as pl
from jax.experimental.pallas import tpu as pltpu
from jax.sharding import PartitionSpec as P

PROX_ITERS = 8
LANES = 128


penalty = 1.0
step_size = 0.08
coupling = 4.0
power_limit = 2.0

VMEM = pl.BlockSpec(memory_space=pltpu.VMEM)
SMEM = pl.BlockSpec(memory_space=pltpu.SMEM)
HBM = pl.BlockSpec(memory_space=pltpu.HBM)
PARAMS = pltpu.CompilerParams(vmem_limit_bytes=12 * 1024 * 1024)


def row_sums(block):
    total = block[:, :LANES]
    for start in range(LANES, block.shape[1], LANES):
        total = total + block[:, start : start + LANES]
    return jnp.sum(total.T, axis=0, keepdims=True)


def fetch(pairs, sems):
    copies = [pltpu.make_async_copy(src, dst, sems.at[i]) for i, (src, dst) in enumerate(pairs)]
    for copy in copies:
        copy.start()
    return copies


def put_sums(sums_ref, x_ref):
    for start in range(0, x_ref.shape[0], LANES):
        block = x_ref[start : start + LANES, :].astype(jnp.float32)
        sums_ref[start // LANES : start // LANES + 1, :] = row_sums(block)


def affine(x, image, gain, fixed):
    return x * gain - (fixed + step_size * image)


def column(row):
    n = row.shape[1]
    down = lax.broadcasted_iota(jnp.int32, (n, n), 0)
    across = lax.broadcasted_iota(jnp.int32, (n, n), 1)
    spread = jnp.broadcast_to(row, (n, n))
    return jnp.sum(jnp.where(down == across, spread, 0.0), axis=1, keepdims=True)


def prep_kernel(
    first_ref, target_hbm, anc_hbm, weight_hbm, mask_hbm, diag_hbm,
    q_hbm, anchor_hbm, cost_hbm, dual_hbm,
    sums_ref, q_out, fixed_out, z_out, gain_out, thin_out,
    target_ref, anc_ref, weight_ref, mask_ref, diag_ref,
    q_ref, anchor_ref, cost_ref, dual_ref, sems,
):
    sources = (
        anc_hbm, weight_hbm, mask_hbm, diag_hbm, target_hbm, anchor_hbm, q_hbm, cost_hbm, dual_hbm
    )
    places = (
        anc_ref, weight_ref, mask_ref, diag_ref, target_ref, anchor_ref, q_ref, cost_ref, dual_ref
    )
    copies = fetch(list(zip(sources, places)), sems)
    copies[0].wait()
    copies[1].wait()
    leaves, sections = anc_ref.shape
    rows_all = leaves * sections
    thin = (sections, LANES)
    first_leaf = first_ref[0].astype(jnp.float32)
    owner_of = anc_ref[...].astype(jnp.float32)
    anc = [jnp.broadcast_to(column(owner_of[i : i + 1, :]), thin) for i in range(leaves)]
    run, same = [], []
    for i in range(leaves):
        weight = jnp.broadcast_to(weight_ref[:, i : i + 1], thin)
        thin_out[3 * rows_all + i * sections : 3 * rows_all + (i + 1) * sections, :] = weight
        same.append(jnp.where(anc[i] == anc[i - 1], 1.0, 0.0) if i else jnp.zeros(thin, jnp.float32))
        run.append(weight + same[i] * run[-1] if i else weight)
    for i in reversed(range(leaves - 1)):
        run[i] = jnp.where(same[i + 1] > 0.5, run[i + 1], run[i])
    for i in range(leaves):
        start = i * sections
        front = jnp.where(anc[i] < first_leaf, 1.0, 0.0)
        thin_out[start : start + sections, :] = same[i]
        thin_out[rows_all + start : rows_all + start + sections, :] = 1.0 / run[i]
        thin_out[2 * rows_all + start : 2 * rows_all + start + sections, :] = jnp.where(
            anc[i] == anc[-1], 2.0, front
        )
    cont = jnp.where(anc[0] < first_leaf, 1.0, 0.0)
    span = jnp.where(anc[-1] < first_leaf, 1.0, 0.0)
    end = 4 * rows_all
    thin_out[end : end + sections, :] = cont
    blocks = 8
    per = sections // 4
    section = lax.broadcasted_iota(jnp.int32, thin, 0)
    lane = lax.broadcasted_iota(jnp.int32, thin, 1)
    for block in range(4):
        place = section - block * per
        inside = (place >= 0) & (place < per)
        line = jnp.where(inside & (lane == place), run[-1], 0.0)
        line = jnp.where(inside & (lane == place + 8), run[0] * cont, line)
        line = jnp.where(inside & (lane == place + 16), span, line)
        spot = end + sections + block
        thin_out[spot : spot + 1, :] = jnp.sum(line, axis=0, keepdims=True)
    thin_out[end + sections + 4 : end + sections + blocks, :] = jnp.zeros((4, LANES), jnp.float32)
    copies[2].wait()
    copies[3].wait()
    copies[4].wait()
    gain = 1.0 - step_size * (2.0 * diag_ref[...] + penalty)
    gain_out[...] = gain

    count = mask_ref.shape[0]
    width = q_ref.shape[0] // count
    keep = mask_ref[...].astype(jnp.float32)
    copies[5].wait()
    put_sums(sums_ref, anchor_ref)
    copies[6].wait()
    for i in range(count):
        for j in range(count):
            rows, cols = slice(i * width, (i + 1) * width), slice(j * width, (j + 1) * width)
            block = jnp.broadcast_to(keep[i : i + 1, j : j + 1], (width, width))
            q_out[rows, cols] = q_ref[rows, cols] * block.astype(jnp.bfloat16)
    image = jnp.dot(anchor_ref[...], q_out[...], preferred_element_type=jnp.float32)
    z_out[...] = image
    copies[7].wait()
    copies[8].wait()
    for i in range(leaves):
        rows = slice(i * sections, (i + 1) * sections)
        pull = (step_size * coupling) * column(target_ref[i : i + 1, :])
        start_pt = anchor_ref[rows, :].astype(jnp.float32)
        linear = cost_ref[rows, :].astype(jnp.float32) + dual_ref[rows, :] - penalty * start_pt
        fixed = step_size * linear - pull
        fixed_out[rows, :] = fixed
        z_out[rows, :] = affine(start_pt, z_out[rows, :], gain, fixed)


def clipped(total_nodes, got_ref, z_ref, x_ref):
    shift = jnp.sum(got_ref[...], axis=0) * (step_size * coupling / total_nodes)
    for i in range(z_ref.shape[0] // LANES):
        rows = slice(i * LANES, (i + 1) * LANES)
        tile = jnp.broadcast_to(shift[i : i + 1, :], (LANES, LANES)).T
        for start in range(0, z_ref.shape[1], LANES):
            cols = slice(start, start + LANES)
            x_ref[rows, cols] = jnp.clip(z_ref[rows, cols] - tile, -power_limit, power_limit)


def step_kernel(
    total_nodes, got_ref, z_ref, q_ref, fixed_ref, gain_ref, sums_ref, z_out, x_ref
):
    clipped(total_nodes, got_ref, z_ref, x_ref)
    put_sums(sums_ref, x_ref)
    x = x_ref[...]
    image = jnp.dot(x.astype(jnp.bfloat16), q_ref[...], preferred_element_type=jnp.float32)
    z_out[...] = affine(x, image, gain_ref[...], fixed_ref[...])


def last_kernel(
    total_nodes, leaves, got_ref, z_ref, thin_ref,
    x_ref, own_ref, sent_ref, tail_ref, head_ref,
):
    clipped(total_nodes, got_ref, z_ref, x_ref)
    rows_all, nodes = x_ref.shape
    sections = rows_all // leaves
    owners = sent_ref.shape[0]
    node_blocks = nodes // LANES
    per = sections * node_blocks // owners
    end = 4 * rows_all
    for start in range(0, nodes, LANES):
        cols = slice(start, start + LANES)
        run = []
        for i in range(leaves):
            rows = slice(i * sections, (i + 1) * sections)
            mine = slice(3 * rows_all + i * sections, 3 * rows_all + (i + 1) * sections)
            term = thin_ref[mine, :] * x_ref[rows, cols]
            run.append(term if i == 0 else term + thin_ref[rows, :] * run[-1])
        total = run[-1]
        tail_ref[:, cols] = total
        for i in reversed(range(leaves)):
            rows = slice(i * sections, (i + 1) * sections)
            if i < leaves - 1:
                later = slice((i + 1) * sections, (i + 2) * sections)
                total = jnp.where(thin_ref[later, :] > 0.5, total, run[i])
            recip = slice(rows_all + i * sections, rows_all + (i + 1) * sections)
            own_ref[rows, cols] = total * thin_ref[recip, :]
        head_ref[:, cols] = total * thin_ref[end : end + sections, :]
    zeros = jnp.zeros((8 - per, LANES), jnp.float32)
    for owner in range(owners):
        block, col = owner // node_blocks, owner % node_blocks
        rows, cols = slice(block * per, (block + 1) * per), slice(col * LANES, (col + 1) * LANES)
        spot = end + sections + block
        sent_ref[owner, 0:per, :] = tail_ref[rows, cols]
        sent_ref[owner, per:8, :] = zeros
        sent_ref[owner, per : per + 1, :] = thin_ref[spot : spot + 1, :]
        sent_ref[owner, 8 : 8 + per, :] = head_ref[rows, cols]
        sent_ref[owner, 8 + per : 16, :] = zeros


def owner_kernel(got_ref, back_ref):
    per = back_ref.shape[1] * back_ref.shape[2] // 2
    groups = got_ref.shape[0]
    shape = (8, LANES)
    tails = [got_ref[g, 0:8, :] for g in range(groups)]
    heads = [got_ref[g, 8:16, :] for g in range(groups)]
    down = lax.broadcasted_iota(jnp.int32, shape, 0)
    across = lax.broadcasted_iota(jnp.int32, shape, 1)

    def scalars(g, first):
        line = jnp.broadcast_to(got_ref[g, per : per + 1, :], shape)
        mine = jnp.where(across == down + first, line, 0.0)
        return jnp.broadcast_to(jnp.sum(mine, axis=1, keepdims=True), shape)

    tail_w = [scalars(g, 0) for g in range(groups)]
    head_w = [scalars(g, 8) for g in range(groups)]
    spans = [scalars(g, 16) for g in range(groups)]
    zero = jnp.zeros(shape, jnp.float32)
    before, before_w, after, after_w = [zero], [zero], [zero], [zero]
    for g in range(groups - 1):
        before.append(tails[g] + spans[g] * before[-1])
        before_w.append(tail_w[g] + spans[g] * before_w[-1])
    for g in reversed(range(1, groups)):
        after.insert(0, heads[g] + spans[g] * after[0])
        after_w.insert(0, head_w[g] + spans[g] * after_w[0])
    for g in range(groups):
        first_w = before_w[g] + head_w[g] + spans[g] * after_w[g]
        last_w = tail_w[g] + after_w[g] + spans[g] * before_w[g]
        first_w = jnp.where(first_w > 0.0, first_w, 1.0)
        last_w = jnp.where(last_w > 0.0, last_w, 1.0)
        first = (before[g] + heads[g] + spans[g] * after[g]) / first_w
        last = (tails[g] + after[g] + spans[g] * before[g]) / last_w
        for i, row in enumerate((first, last)):
            for j in range(per):
                spot = i * per + j
                back_ref[g, spot // 4, spot % 4 : spot % 4 + 1, :] = row[j : j + 1]


def final_kernel(
    got_ref, own_ref, thin_ref, x_ref, dual_ref, x_hbm, average_hbm, new_dual_hbm,
    first_ref, last_ref, average_ref, new_dual_ref, sems, x_sem,
):
    copies = [pltpu.make_async_copy(x_ref, x_hbm, x_sem)]
    copies[0].start()
    owners = got_ref.shape[0]
    sections, nodes = first_ref.shape
    node_blocks = nodes // LANES
    per = sections * node_blocks // owners
    for owner in range(owners):
        block, col = owner // node_blocks, owner % node_blocks
        cols = slice(col * LANES, (col + 1) * LANES)
        for i, edge_ref in enumerate((first_ref, last_ref)):
            for j in range(per):
                spot, row = i * per + j, block * per + j
                edge_ref[row : row + 1, cols] = got_ref[owner, spot // 4, spot % 4 : spot % 4 + 1, :]
    leaves = x_ref.shape[0] // sections
    chunks = sems.shape[1]
    each = leaves // chunks
    for chunk in range(chunks):
        for i in range(chunk * each, (chunk + 1) * each):
            rows = slice(i * sections, (i + 1) * sections)
            offset = 2 * leaves * sections + i * sections
            pick = thin_ref[offset : offset + sections, :]
            for start in range(0, nodes, LANES):
                cols = slice(start, start + LANES)
                ends = jnp.where(pick > 1.5, last_ref[:, cols], first_ref[:, cols])
                average = jnp.where(pick > 0.5, ends, own_ref[rows, cols])
                average_ref[rows, cols] = average
                new_dual_ref[rows, cols] = dual_ref[rows, cols] + penalty * (
                    x_ref[rows, cols] - average
                )
        part = pl.ds(chunk * each * sections, each * sections)
        for n, (src, dst) in enumerate(((average_ref, average_hbm), (new_dual_ref, new_dual_hbm))):
            copy = pltpu.make_async_copy(src.at[part, :], dst.at[part, :], sems.at[n, chunk])
            copy.start()
            copies.append(copy)
    for copy in copies:
        copy.wait()


def call(kernel, inputs, outputs, in_specs=None, out_specs=None, scratch=(), name=None):
    return pl.pallas_call(
        kernel,
        out_shape=outputs,
        in_specs=in_specs or [VMEM] * len(inputs),
        out_specs=out_specs or jax.tree.map(lambda _: VMEM, outputs),
        scratch_shapes=scratch,
        compiler_params=PARAMS,
        name=name,
    )(*inputs)


def shaped(shape, dtype=jnp.float32):
    return jax.ShapeDtypeStruct(shape, dtype)


def far(array):
    return pltpu.with_memory_space_constraint(array, pltpu.HBM)


def gather_parts(part):
    spread = jnp.broadcast_to(part, (lax.axis_size("feeder"),) + part.shape)
    return lax.all_to_all(spread, "feeder", 0, 0)


def local(anchor, cost_lin, dual, target, leaf_weight, q_mat, diag_gain, block_mask, ancestor):
    leaves, sections, nodes = anchor.shape
    rows = leaves * sections
    groups = lax.axis_size("scen")
    total_nodes = lax.axis_size("feeder") * nodes
    flat = lambda a: a.reshape(rows, nodes)
    sums_shape = shaped((rows // LANES, LANES))
    full, small = shaped((rows, nodes)), shaped((4 * rows + sections + 8, LANES))
    buffer = pltpu.VMEM((rows, nodes), jnp.float32)
    edge = pltpu.VMEM((sections, nodes), jnp.float32)

    first_leaf = (lax.axis_index("scen") * leaves).astype(jnp.int32).reshape(1)
    small_args = (
        target, ancestor.T, leaf_weight.reshape(1, leaves), block_mask[0],
        diag_gain.reshape(1, nodes),
    )
    large_args = (q_mat, flat(anchor), flat(cost_lin), flat(dual))
    sums, q_eff, fixed, z, gain, thin = call(
        prep_kernel,
        (first_leaf,) + tuple(far(a) for a in small_args + large_args),
        (sums_shape, shaped((nodes, nodes), jnp.bfloat16), full, full, shaped((1, nodes)), small),
        in_specs=[SMEM] + [HBM] * 9,
        scratch=tuple(pltpu.VMEM(a.shape, a.dtype) for a in small_args + large_args)
        + (pltpu.SemaphoreType.DMA((9,)),),
        name="prep",
    )
    got = gather_parts(sums)
    for sweep in range(PROX_ITERS - 1):
        sums, z = call(
            lambda *refs: step_kernel(total_nodes, *refs),
            (got, z, q_eff, fixed, gain),
            (sums_shape, full),
            scratch=(buffer,),
            name="prox_step",
        )
        got = gather_parts(sums)
    x, own, sent = call(
        lambda *refs: last_kernel(total_nodes, leaves, *refs),
        (got, z, thin),
        (full, full, shaped((groups, 16, LANES))),
        scratch=(edge, edge),
        name="last_step",
    )
    per = sections * (nodes // LANES) // groups
    got = lax.all_to_all(sent, "scen", 0, 0)
    back = call(owner_kernel, (got,), shaped((groups, per // 2, 4, LANES)), name="owner_chain")
    got = lax.all_to_all(back, "scen", 0, 0)
    x, average, new_dual = call(
        final_kernel,
        (got, own, thin, x, flat(dual)),
        (full, full, full),
        out_specs=(HBM, HBM, HBM),
        scratch=(
            edge, edge, buffer, buffer, pltpu.SemaphoreType.DMA((2, 4)), pltpu.SemaphoreType.DMA
        ),
        name="finish",
    )
    whole = lambda a: a.reshape(leaves, sections, nodes)
    return (whole(x), whole(average), whole(new_dual))


def solution(mesh):
    return jax.shard_map(
        local,
        mesh=mesh,
        in_specs=(
            P("scen", None, "feeder"),
            P("scen", None, "feeder"),
            P("scen", None, "feeder"),
            P("scen", None),
            P("scen"),
            P("feeder", None),
            P("feeder"),
            P("feeder", None, None),
            P(None, "scen"),
        ),
        out_specs=(P("scen", None, "feeder"), P("scen", None, "feeder"), P("scen", None, "feeder")),
        check_vma=False,
    )
```

```python
import jax
import jax.numpy as jnp
from jax import lax
from jax.experimental import pallas as pl
from jax.experimental.pallas import tpu as pltpu
from jax.sharding import PartitionSpec as P

PROX_ITERS = 8
LANES = 128


penalty = 1.0
step_size = 0.08
coupling = 4.0
power_limit = 2.0

VMEM = pl.BlockSpec(memory_space=pltpu.VMEM)
SMEM = pl.BlockSpec(memory_space=pltpu.SMEM)
HBM = pl.BlockSpec(memory_space=pltpu.HBM)
PARAMS = pltpu.CompilerParams(vmem_limit_bytes=12 * 1024 * 1024)


def row_sums(block):
    total = block[:, :LANES]
    for start in range(LANES, block.shape[1], LANES):
        total = total + block[:, start : start + LANES]
    return jnp.sum(total.T, axis=0, keepdims=True)


def fetch(pairs, sems):
    copies = [pltpu.make_async_copy(src, dst, sems.at[i]) for i, (src, dst) in enumerate(pairs)]
    for copy in copies:
        copy.start()
    return copies


def sum_kernel(anchor_hbm, spread_ref, anchor_ref, sems):
    parts = [pl.ds(i * LANES, LANES) for i in range(anchor_ref.shape[0] // LANES)]
    copies = fetch([(anchor_hbm.at[part, :], anchor_ref.at[part, :]) for part in parts], sems)
    for i, part in enumerate(parts):
        copies[i].wait()
        total = row_sums(anchor_ref[part, :].astype(jnp.float32))
        for feeder in range(spread_ref.shape[0]):
            spread_ref[feeder, i : i + 1, :] = total


def affine(x, image, gain, fixed):
    return x * gain - (fixed + step_size * image)


def column(row):
    n = row.shape[1]
    down = lax.broadcasted_iota(jnp.int32, (n, n), 0)
    across = lax.broadcasted_iota(jnp.int32, (n, n), 1)
    spread = jnp.broadcast_to(row, (n, n))
    return jnp.sum(jnp.where(down == across, spread, 0.0), axis=1, keepdims=True)


def prep_kernel(
    first_ref, target_hbm, anc_hbm, weight_hbm, mask_hbm, diag_hbm,
    q_hbm, anchor_hbm, cost_hbm, dual_hbm,
    q_out, fixed_out, z_out, gain_out, thin_out,
    target_ref, anc_ref, weight_ref, mask_ref, diag_ref,
    q_ref, anchor_ref, cost_ref, dual_ref, sems,
):
    sources = (
        anc_hbm, weight_hbm, mask_hbm, diag_hbm, target_hbm, q_hbm, anchor_hbm, cost_hbm, dual_hbm
    )
    places = (
        anc_ref, weight_ref, mask_ref, diag_ref, target_ref, q_ref, anchor_ref, cost_ref, dual_ref
    )
    copies = fetch(list(zip(sources, places)), sems)
    copies[0].wait()
    copies[1].wait()
    leaves, sections = anc_ref.shape
    rows_all = leaves * sections
    thin = (sections, LANES)
    first_leaf = first_ref[0].astype(jnp.float32)
    owner_of = anc_ref[...].astype(jnp.float32)
    anc = [jnp.broadcast_to(column(owner_of[i : i + 1, :]), thin) for i in range(leaves)]
    run, same = [], []
    for i in range(leaves):
        weight = jnp.broadcast_to(weight_ref[:, i : i + 1], thin)
        thin_out[3 * rows_all + i * sections : 3 * rows_all + (i + 1) * sections, :] = weight
        same.append(jnp.where(anc[i] == anc[i - 1], 1.0, 0.0) if i else jnp.zeros(thin, jnp.float32))
        run.append(weight + same[i] * run[-1] if i else weight)
    for i in reversed(range(leaves - 1)):
        run[i] = jnp.where(same[i + 1] > 0.5, run[i + 1], run[i])
    for i in range(leaves):
        start = i * sections
        front = jnp.where(anc[i] < first_leaf, 1.0, 0.0)
        thin_out[start : start + sections, :] = same[i]
        thin_out[rows_all + start : rows_all + start + sections, :] = 1.0 / run[i]
        thin_out[2 * rows_all + start : 2 * rows_all + start + sections, :] = jnp.where(
            anc[i] == anc[-1], 2.0, front
        )
    cont = jnp.where(anc[0] < first_leaf, 1.0, 0.0)
    span = jnp.where(anc[-1] < first_leaf, 1.0, 0.0)
    end = 4 * rows_all
    thin_out[end : end + sections, :] = cont
    blocks = 8
    per = sections // 4
    section = lax.broadcasted_iota(jnp.int32, thin, 0)
    lane = lax.broadcasted_iota(jnp.int32, thin, 1)
    for block in range(4):
        place = section - block * per
        inside = (place >= 0) & (place < per)
        line = jnp.where(inside & (lane == place), run[-1], 0.0)
        line = jnp.where(inside & (lane == place + 8), run[0] * cont, line)
        line = jnp.where(inside & (lane == place + 16), span, line)
        spot = end + sections + block
        thin_out[spot : spot + 1, :] = jnp.sum(line, axis=0, keepdims=True)
    thin_out[end + sections + 4 : end + sections + blocks, :] = jnp.zeros((4, LANES), jnp.float32)
    copies[2].wait()
    copies[3].wait()
    copies[4].wait()
    gain = 1.0 - step_size * (2.0 * diag_ref[...] + penalty)
    gain_out[...] = gain

    count = mask_ref.shape[0]
    width = q_ref.shape[0] // count
    keep = mask_ref[...].astype(jnp.float32)
    copies[5].wait()
    for i in range(count):
        for j in range(count):
            rows, cols = slice(i * width, (i + 1) * width), slice(j * width, (j + 1) * width)
            block = jnp.broadcast_to(keep[i : i + 1, j : j + 1], (width, width))
            q_out[rows, cols] = q_ref[rows, cols] * block.astype(jnp.bfloat16)
    copies[6].wait()
    image = jnp.dot(anchor_ref[...], q_out[...], preferred_element_type=jnp.float32)
    z_out[...] = image
    copies[7].wait()
    copies[8].wait()
    for i in range(leaves):
        rows = slice(i * sections, (i + 1) * sections)
        pull = (step_size * coupling) * column(target_ref[i : i + 1, :])
        start_pt = anchor_ref[rows, :].astype(jnp.float32)
        linear = cost_ref[rows, :].astype(jnp.float32) + dual_ref[rows, :] - penalty * start_pt
        fixed = step_size * linear - pull
        fixed_out[rows, :] = fixed
        z_out[rows, :] = affine(start_pt, z_out[rows, :], gain, fixed)


def clipped(total_nodes, got_ref, z_ref, x_ref):
    shift = jnp.sum(got_ref[...], axis=0) * (step_size * coupling / total_nodes)
    for i in range(z_ref.shape[0] // LANES):
        rows = slice(i * LANES, (i + 1) * LANES)
        tile = jnp.broadcast_to(shift[i : i + 1, :], (LANES, LANES)).T
        for start in range(0, z_ref.shape[1], LANES):
            cols = slice(start, start + LANES)
            x_ref[rows, cols] = jnp.clip(z_ref[rows, cols] - tile, -power_limit, power_limit)


def step_kernel(
    total_nodes, got_ref, z_ref, q_ref, fixed_ref, gain_ref, sums_ref, z_out, x_ref
):
    clipped(total_nodes, got_ref, z_ref, x_ref)
    for i in range(x_ref.shape[0] // LANES):
        sums_ref[i : i + 1, :] = row_sums(x_ref[i * LANES : (i + 1) * LANES, :])
    x = x_ref[...]
    image = jnp.dot(x.astype(jnp.bfloat16), q_ref[...], preferred_element_type=jnp.float32)
    z_out[...] = affine(x, image, gain_ref[...], fixed_ref[...])


def last_kernel(
    total_nodes, leaves, got_ref, z_ref, thin_ref,
    x_ref, own_ref, sent_ref, tail_ref, head_ref,
):
    clipped(total_nodes, got_ref, z_ref, x_ref)
    rows_all, nodes = x_ref.shape
    sections = rows_all // leaves
    owners = sent_ref.shape[0]
    node_blocks = nodes // LANES
    per = sections * node_blocks // owners
    end = 4 * rows_all
    for start in range(0, nodes, LANES):
        cols = slice(start, start + LANES)
        run = []
        for i in range(leaves):
            rows = slice(i * sections, (i + 1) * sections)
            mine = slice(3 * rows_all + i * sections, 3 * rows_all + (i + 1) * sections)
            term = thin_ref[mine, :] * x_ref[rows, cols]
            run.append(term if i == 0 else term + thin_ref[rows, :] * run[-1])
        total = run[-1]
        tail_ref[:, cols] = total
        for i in reversed(range(leaves)):
            rows = slice(i * sections, (i + 1) * sections)
            if i < leaves - 1:
                later = slice((i + 1) * sections, (i + 2) * sections)
                total = jnp.where(thin_ref[later, :] > 0.5, total, run[i])
            recip = slice(rows_all + i * sections, rows_all + (i + 1) * sections)
            own_ref[rows, cols] = total * thin_ref[recip, :]
        head_ref[:, cols] = total * thin_ref[end : end + sections, :]
    for owner in range(owners):
        block, col = owner // node_blocks, owner % node_blocks
        cols = slice(col * LANES, (col + 1) * LANES)
        spot = end + sections + block
        lines = [(ref, block * per + j, cols) for ref in (tail_ref, head_ref) for j in range(per)]
        for j, (ref, row, part) in enumerate(lines + [(thin_ref, spot, slice(0, LANES))]):
            sent_ref[owner, :, j * LANES : (j + 1) * LANES] = ref[row : row + 1, part]


def owner_kernel(got_ref, back_ref, tile_ref):
    per = back_ref.shape[1] * back_ref.shape[2] // 2
    groups = got_ref.shape[0]
    shape = (8, LANES)
    for g in range(groups):
        for j in range(2 * per):
            spot = j if j < per else 8 + j - per
            tile_ref[g, spot : spot + 1, :] = got_ref[g, :, j * LANES : (j + 1) * LANES]
    zeros = jnp.zeros((8 - per, LANES), jnp.float32)
    for g in range(groups):
        tile_ref[g, per:8, :] = zeros
        tile_ref[g, 8 + per : 16, :] = zeros
    tails = [tile_ref[g, 0:8, :] for g in range(groups)]
    heads = [tile_ref[g, 8:16, :] for g in range(groups)]
    down = lax.broadcasted_iota(jnp.int32, shape, 0)
    across = lax.broadcasted_iota(jnp.int32, shape, 1)

    def scalars(g, first):
        line = jnp.broadcast_to(got_ref[g, :, 2 * per * LANES :], shape)
        mine = jnp.where(across == down + first, line, 0.0)
        return jnp.broadcast_to(jnp.sum(mine, axis=1, keepdims=True), shape)

    tail_w = [scalars(g, 0) for g in range(groups)]
    head_w = [scalars(g, 8) for g in range(groups)]
    spans = [scalars(g, 16) for g in range(groups)]
    zero = jnp.zeros(shape, jnp.float32)
    before, before_w, after, after_w = [zero], [zero], [zero], [zero]
    for g in range(groups - 1):
        before.append(tails[g] + spans[g] * before[-1])
        before_w.append(tail_w[g] + spans[g] * before_w[-1])
    for g in reversed(range(1, groups)):
        after.insert(0, heads[g] + spans[g] * after[0])
        after_w.insert(0, head_w[g] + spans[g] * after_w[0])
    for g in range(groups):
        first_w = before_w[g] + head_w[g] + spans[g] * after_w[g]
        last_w = tail_w[g] + after_w[g] + spans[g] * before_w[g]
        first_w = jnp.where(first_w > 0.0, first_w, 1.0)
        last_w = jnp.where(last_w > 0.0, last_w, 1.0)
        first = (before[g] + heads[g] + spans[g] * after[g]) / first_w
        last = (tails[g] + after[g] + spans[g] * before[g]) / last_w
        for i, row in enumerate((first, last)):
            for j in range(per):
                spot = i * per + j
                back_ref[g, spot // 4, spot % 4 : spot % 4 + 1, :] = row[j : j + 1]


def final_kernel(
    got_ref, own_ref, thin_ref, x_ref, dual_ref, x_hbm, average_hbm, new_dual_hbm,
    first_ref, last_ref, average_ref, new_dual_ref, sems, x_sem,
):
    copies = [pltpu.make_async_copy(x_ref, x_hbm, x_sem)]
    copies[0].start()
    owners = got_ref.shape[0]
    sections, nodes = first_ref.shape
    node_blocks = nodes // LANES
    per = sections * node_blocks // owners
    for owner in range(owners):
        block, col = owner // node_blocks, owner % node_blocks
        cols = slice(col * LANES, (col + 1) * LANES)
        for i, edge_ref in enumerate((first_ref, last_ref)):
            for j in range(per):
                spot, row = i * per + j, block * per + j
                edge_ref[row : row + 1, cols] = got_ref[owner, spot // 4, spot % 4 : spot % 4 + 1, :]
    leaves = x_ref.shape[0] // sections
    chunks = sems.shape[1]
    each = leaves // chunks
    for chunk in range(chunks):
        for i in range(chunk * each, (chunk + 1) * each):
            rows = slice(i * sections, (i + 1) * sections)
            offset = 2 * leaves * sections + i * sections
            pick = thin_ref[offset : offset + sections, :]
            for start in range(0, nodes, LANES):
                cols = slice(start, start + LANES)
                ends = jnp.where(pick > 1.5, last_ref[:, cols], first_ref[:, cols])
                average = jnp.where(pick > 0.5, ends, own_ref[rows, cols])
                average_ref[rows, cols] = average
                new_dual_ref[rows, cols] = dual_ref[rows, cols] + penalty * (
                    x_ref[rows, cols] - average
                )
        part = pl.ds(chunk * each * sections, each * sections)
        for n, (src, dst) in enumerate(((average_ref, average_hbm), (new_dual_ref, new_dual_hbm))):
            copy = pltpu.make_async_copy(src.at[part, :], dst.at[part, :], sems.at[n, chunk])
            copy.start()
            copies.append(copy)
    for copy in copies:
        copy.wait()


def call(kernel, inputs, outputs, in_specs=None, out_specs=None, scratch=(), name=None):
    return pl.pallas_call(
        kernel,
        out_shape=outputs,
        in_specs=in_specs or [VMEM] * len(inputs),
        out_specs=out_specs or jax.tree.map(lambda _: VMEM, outputs),
        scratch_shapes=scratch,
        compiler_params=PARAMS,
        name=name,
    )(*inputs)


def shaped(shape, dtype=jnp.float32):
    return jax.ShapeDtypeStruct(shape, dtype)


def far(array):
    return pltpu.with_memory_space_constraint(array, pltpu.HBM)


def gather_parts(part):
    spread = jnp.broadcast_to(part, (lax.axis_size("feeder"),) + part.shape)
    return lax.all_to_all(spread, "feeder", 0, 0)


def local(anchor, cost_lin, dual, target, leaf_weight, q_mat, diag_gain, block_mask, ancestor):
    leaves, sections, nodes = anchor.shape
    rows = leaves * sections
    groups = lax.axis_size("scen")
    total_nodes = lax.axis_size("feeder") * nodes
    flat = lambda a: a.reshape(rows, nodes)
    sums_shape = shaped((rows // LANES, LANES))
    full, small = shaped((rows, nodes)), shaped((4 * rows + sections + 8, LANES))
    buffer = pltpu.VMEM((rows, nodes), jnp.float32)
    edge = pltpu.VMEM((sections, nodes), jnp.float32)

    narrow = pltpu.VMEM((rows, nodes), jnp.bfloat16)
    spread = call(
        sum_kernel,
        (far(flat(anchor)),),
        shaped((lax.axis_size("feeder"),) + sums_shape.shape),
        in_specs=[HBM],
        scratch=(narrow, pltpu.SemaphoreType.DMA((rows // LANES,))),
        name="start_sums",
    )
    got = lax.all_to_all(spread, "feeder", 0, 0)
    first_leaf = (lax.axis_index("scen") * leaves).astype(jnp.int32).reshape(1)
    small_args = (
        target, ancestor.T, leaf_weight.reshape(1, leaves), block_mask[0],
        diag_gain.reshape(1, nodes),
    )
    large_args = (q_mat, flat(anchor), flat(cost_lin), flat(dual))
    q_eff, fixed, z, gain, thin = call(
        prep_kernel,
        (first_leaf,) + tuple(far(a) for a in small_args + large_args),
        (shaped((nodes, nodes), jnp.bfloat16), full, full, shaped((1, nodes)), small),
        in_specs=[SMEM] + [HBM] * 9,
        scratch=tuple(pltpu.VMEM(a.shape, a.dtype) for a in small_args + large_args)
        + (pltpu.SemaphoreType.DMA((9,)),),
        name="prep",
    )
    for sweep in range(PROX_ITERS - 1):
        sums, z = call(
            lambda *refs: step_kernel(total_nodes, *refs),
            (got, z, q_eff, fixed, gain),
            (sums_shape, full),
            scratch=(buffer,),
            name="prox_step",
        )
        got = gather_parts(sums)
    per = sections * (nodes // LANES) // groups
    x, own, sent = call(
        lambda *refs: last_kernel(total_nodes, leaves, *refs),
        (got, z, thin),
        (full, full, shaped((groups, 1, (2 * per + 1) * LANES))),
        scratch=(edge, edge),
        name="last_step",
    )
    got = lax.all_to_all(sent, "scen", 0, 0)
    back = call(owner_kernel, (got,), shaped((groups, per // 2, 4, LANES)),
                scratch=(pltpu.VMEM((groups, 16, LANES), jnp.float32),), name="owner_chain")
    got = lax.all_to_all(back, "scen", 0, 0)
    x, average, new_dual = call(
        final_kernel,
        (got, own, thin, x, flat(dual)),
        (full, full, full),
        out_specs=(HBM, HBM, HBM),
        scratch=(
            edge, edge, buffer, buffer, pltpu.SemaphoreType.DMA((2, 4)), pltpu.SemaphoreType.DMA
        ),
        name="finish",
    )
    whole = lambda a: a.reshape(leaves, sections, nodes)
    return (whole(x), whole(average), whole(new_dual))


def solution(mesh):
    return jax.shard_map(
        local,
        mesh=mesh,
        in_specs=(
            P("scen", None, "feeder"),
            P("scen", None, "feeder"),
            P("scen", None, "feeder"),
            P("scen", None),
            P("scen"),
            P("feeder", None),
            P("feeder"),
            P("feeder", None, None),
            P(None, "scen"),
        ),
        out_specs=(P("scen", None, "feeder"), P("scen", None, "feeder"), P("scen", None, "feeder")),
        check_vma=False,
    )
```

```python
import jax
import jax.numpy as jnp
from jax import lax
from jax.experimental import pallas as pl
from jax.experimental.pallas import tpu as pltpu
from jax.sharding import PartitionSpec as P

PROX_ITERS = 8
LANES = 128


penalty = 1.0
step_size = 0.08
coupling = 4.0
power_limit = 2.0

VMEM = pl.BlockSpec(memory_space=pltpu.VMEM)
SMEM = pl.BlockSpec(memory_space=pltpu.SMEM)
HBM = pl.BlockSpec(memory_space=pltpu.HBM)
PARAMS = pltpu.CompilerParams(vmem_limit_bytes=12 * 1024 * 1024)


def row_sums(block):
    total = block[:, :LANES]
    for start in range(LANES, block.shape[1], LANES):
        total = total + block[:, start : start + LANES]
    return jnp.sum(total.T, axis=0, keepdims=True)


def fetch(pairs, sems):
    copies = [pltpu.make_async_copy(src, dst, sems.at[i]) for i, (src, dst) in enumerate(pairs)]
    for copy in copies:
        copy.start()
    return copies


def put_spread(spread_ref, i, line):
    for feeder in range(spread_ref.shape[0]):
        spread_ref[feeder, :, i * LANES : (i + 1) * LANES] = line


def sum_kernel(anchor_hbm, spread_ref, anchor_ref, sems):
    parts = [pl.ds(i * LANES, LANES) for i in range(anchor_ref.shape[0] // LANES)]
    copies = fetch([(anchor_hbm.at[part, :], anchor_ref.at[part, :]) for part in parts], sems)
    for i, part in enumerate(parts):
        copies[i].wait()
        total = row_sums(anchor_ref[part, :].astype(jnp.float32))
        put_spread(spread_ref, i, total)


def affine(x, image, gain, fixed):
    return x * gain - (fixed + step_size * image)


def column(row):
    n = row.shape[1]
    down = lax.broadcasted_iota(jnp.int32, (n, n), 0)
    across = lax.broadcasted_iota(jnp.int32, (n, n), 1)
    spread = jnp.broadcast_to(row, (n, n))
    return jnp.sum(jnp.where(down == across, spread, 0.0), axis=1, keepdims=True)


def prep_kernel(
    first_ref, target_hbm, anc_hbm, weight_hbm, mask_hbm, diag_hbm,
    q_hbm, anchor_hbm, cost_hbm, dual_hbm,
    q_out, fixed_out, z_out, gain_out, thin_out,
    target_ref, anc_ref, weight_ref, mask_ref, diag_ref,
    q_ref, anchor_ref, cost_ref, dual_ref, sems,
):
    sources = (
        anc_hbm, weight_hbm, mask_hbm, diag_hbm, target_hbm, q_hbm, anchor_hbm, cost_hbm, dual_hbm
    )
    places = (
        anc_ref, weight_ref, mask_ref, diag_ref, target_ref, q_ref, anchor_ref, cost_ref, dual_ref
    )
    copies = fetch(list(zip(sources, places)), sems)
    copies[0].wait()
    copies[1].wait()
    leaves, sections = anc_ref.shape
    rows_all = leaves * sections
    thin = (sections, LANES)
    first_leaf = first_ref[0].astype(jnp.float32)
    owner_of = anc_ref[...].astype(jnp.float32)
    anc = [jnp.broadcast_to(column(owner_of[i : i + 1, :]), thin) for i in range(leaves)]
    run, same = [], []
    for i in range(leaves):
        weight = jnp.broadcast_to(weight_ref[:, i : i + 1], thin)
        thin_out[3 * rows_all + i * sections : 3 * rows_all + (i + 1) * sections, :] = weight
        same.append(jnp.where(anc[i] == anc[i - 1], 1.0, 0.0) if i else jnp.zeros(thin, jnp.float32))
        run.append(weight + same[i] * run[-1] if i else weight)
    for i in reversed(range(leaves - 1)):
        run[i] = jnp.where(same[i + 1] > 0.5, run[i + 1], run[i])
    for i in range(leaves):
        start = i * sections
        front = jnp.where(anc[i] < first_leaf, 1.0, 0.0)
        thin_out[start : start + sections, :] = same[i]
        thin_out[rows_all + start : rows_all + start + sections, :] = 1.0 / run[i]
        thin_out[2 * rows_all + start : 2 * rows_all + start + sections, :] = jnp.where(
            anc[i] == anc[-1], 2.0, front
        )
    cont = jnp.where(anc[0] < first_leaf, 1.0, 0.0)
    span = jnp.where(anc[-1] < first_leaf, 1.0, 0.0)
    end = 4 * rows_all
    thin_out[end : end + sections, :] = cont
    blocks = 8
    per = sections // 4
    section = lax.broadcasted_iota(jnp.int32, thin, 0)
    lane = lax.broadcasted_iota(jnp.int32, thin, 1)
    for block in range(4):
        place = section - block * per
        inside = (place >= 0) & (place < per)
        line = jnp.where(inside & (lane == place), run[-1], 0.0)
        line = jnp.where(inside & (lane == place + 8), run[0] * cont, line)
        line = jnp.where(inside & (lane == place + 16), span, line)
        spot = end + sections + block
        thin_out[spot : spot + 1, :] = jnp.sum(line, axis=0, keepdims=True)
    thin_out[end + sections + 4 : end + sections + blocks, :] = jnp.zeros((4, LANES), jnp.float32)
    copies[2].wait()
    copies[3].wait()
    copies[4].wait()
    gain = 1.0 - step_size * (2.0 * diag_ref[...] + penalty)
    gain_out[...] = gain

    count = mask_ref.shape[0]
    width = q_ref.shape[0] // count
    keep = mask_ref[...].astype(jnp.float32)
    copies[5].wait()
    for i in range(count):
        for j in range(count):
            rows, cols = slice(i * width, (i + 1) * width), slice(j * width, (j + 1) * width)
            block = jnp.broadcast_to(keep[i : i + 1, j : j + 1], (width, width))
            q_out[rows, cols] = q_ref[rows, cols] * block.astype(jnp.bfloat16)
    copies[6].wait()
    image = jnp.dot(anchor_ref[...], q_out[...], preferred_element_type=jnp.float32)
    z_out[...] = image
    copies[7].wait()
    copies[8].wait()
    for i in range(leaves):
        rows = slice(i * sections, (i + 1) * sections)
        pull = (step_size * coupling) * column(target_ref[i : i + 1, :])
        start_pt = anchor_ref[rows, :].astype(jnp.float32)
        linear = cost_ref[rows, :].astype(jnp.float32) + dual_ref[rows, :] - penalty * start_pt
        fixed = step_size * linear - pull
        fixed_out[rows, :] = fixed
        z_out[rows, :] = affine(start_pt, z_out[rows, :], gain, fixed)


def clipped(total_nodes, got_ref, z_ref, x_ref):
    shift = jnp.sum(got_ref[...], axis=0) * (step_size * coupling / total_nodes)
    for i in range(z_ref.shape[0] // LANES):
        rows = slice(i * LANES, (i + 1) * LANES)
        tile = jnp.broadcast_to(shift[:, rows], (LANES, LANES)).T
        for start in range(0, z_ref.shape[1], LANES):
            cols = slice(start, start + LANES)
            x_ref[rows, cols] = jnp.clip(z_ref[rows, cols] - tile, -power_limit, power_limit)


def step_kernel(
    total_nodes, got_ref, z_ref, q_ref, fixed_ref, gain_ref, spread_ref, z_out, x_ref
):
    clipped(total_nodes, got_ref, z_ref, x_ref)
    for i in range(x_ref.shape[0] // LANES):
        put_spread(spread_ref, i, row_sums(x_ref[i * LANES : (i + 1) * LANES, :]))
    x = x_ref[...]
    image = jnp.dot(x.astype(jnp.bfloat16), q_ref[...], preferred_element_type=jnp.float32)
    z_out[...] = affine(x, image, gain_ref[...], fixed_ref[...])


def last_kernel(
    total_nodes, leaves, got_ref, z_ref, thin_ref,
    x_ref, own_ref, sent_ref, tail_ref, head_ref,
):
    clipped(total_nodes, got_ref, z_ref, x_ref)
    rows_all, nodes = x_ref.shape
    sections = rows_all // leaves
    owners = sent_ref.shape[0]
    node_blocks = nodes // LANES
    per = sections * node_blocks // owners
    end = 4 * rows_all
    for start in range(0, nodes, LANES):
        cols = slice(start, start + LANES)
        run = []
        for i in range(leaves):
            rows = slice(i * sections, (i + 1) * sections)
            mine = slice(3 * rows_all + i * sections, 3 * rows_all + (i + 1) * sections)
            term = thin_ref[mine, :] * x_ref[rows, cols]
            run.append(term if i == 0 else term + thin_ref[rows, :] * run[-1])
        total = run[-1]
        tail_ref[:, cols] = total
        for i in reversed(range(leaves)):
            rows = slice(i * sections, (i + 1) * sections)
            if i < leaves - 1:
                later = slice((i + 1) * sections, (i + 2) * sections)
                total = jnp.where(thin_ref[later, :] > 0.5, total, run[i])
            recip = slice(rows_all + i * sections, rows_all + (i + 1) * sections)
            own_ref[rows, cols] = total * thin_ref[recip, :]
        head_ref[:, cols] = total * thin_ref[end : end + sections, :]
    for owner in range(owners):
        block, col = owner // node_blocks, owner % node_blocks
        cols = slice(col * LANES, (col + 1) * LANES)
        spot = end + sections + block
        lines = [(ref, block * per + j, cols) for ref in (tail_ref, head_ref) for j in range(per)]
        for j, (ref, row, part) in enumerate(lines + [(thin_ref, spot, slice(0, LANES))]):
            sent_ref[owner, :, j * LANES : (j + 1) * LANES] = ref[row : row + 1, part]


def owner_kernel(got_ref, back_ref, tile_ref):
    per = back_ref.shape[1] * back_ref.shape[2] // 2
    groups = got_ref.shape[0]
    shape = (8, LANES)
    for g in range(groups):
        for j in range(2 * per):
            spot = j if j < per else 8 + j - per
            tile_ref[g, spot : spot + 1, :] = got_ref[g, :, j * LANES : (j + 1) * LANES]
    zeros = jnp.zeros((8 - per, LANES), jnp.float32)
    for g in range(groups):
        tile_ref[g, per:8, :] = zeros
        tile_ref[g, 8 + per : 16, :] = zeros
    tails = [tile_ref[g, 0:8, :] for g in range(groups)]
    heads = [tile_ref[g, 8:16, :] for g in range(groups)]
    down = lax.broadcasted_iota(jnp.int32, shape, 0)
    across = lax.broadcasted_iota(jnp.int32, shape, 1)

    def scalars(g, first):
        line = jnp.broadcast_to(got_ref[g, :, 2 * per * LANES :], shape)
        mine = jnp.where(across == down + first, line, 0.0)
        return jnp.broadcast_to(jnp.sum(mine, axis=1, keepdims=True), shape)

    tail_w = [scalars(g, 0) for g in range(groups)]
    head_w = [scalars(g, 8) for g in range(groups)]
    spans = [scalars(g, 16) for g in range(groups)]
    zero = jnp.zeros(shape, jnp.float32)
    before, before_w, after, after_w = [zero], [zero], [zero], [zero]
    for g in range(groups - 1):
        before.append(tails[g] + spans[g] * before[-1])
        before_w.append(tail_w[g] + spans[g] * before_w[-1])
    for g in reversed(range(1, groups)):
        after.insert(0, heads[g] + spans[g] * after[0])
        after_w.insert(0, head_w[g] + spans[g] * after_w[0])
    for g in range(groups):
        first_w = before_w[g] + head_w[g] + spans[g] * after_w[g]
        last_w = tail_w[g] + after_w[g] + spans[g] * before_w[g]
        first_w = jnp.where(first_w > 0.0, first_w, 1.0)
        last_w = jnp.where(last_w > 0.0, last_w, 1.0)
        first = (before[g] + heads[g] + spans[g] * after[g]) / first_w
        last = (tails[g] + after[g] + spans[g] * before[g]) / last_w
        for i, row in enumerate((first, last)):
            for j in range(per):
                spot = i * per + j
                back_ref[g, spot // 4, spot % 4 : spot % 4 + 1, :] = row[j : j + 1]


def final_kernel(
    got_ref, own_ref, thin_ref, x_ref, dual_ref, x_hbm, average_hbm, new_dual_hbm,
    first_ref, last_ref, average_ref, new_dual_ref, sems, x_sem,
):
    copies = [pltpu.make_async_copy(x_ref, x_hbm, x_sem)]
    copies[0].start()
    owners = got_ref.shape[0]
    sections, nodes = first_ref.shape
    node_blocks = nodes // LANES
    per = sections * node_blocks // owners
    for owner in range(owners):
        block, col = owner // node_blocks, owner % node_blocks
        cols = slice(col * LANES, (col + 1) * LANES)
        for i, edge_ref in enumerate((first_ref, last_ref)):
            for j in range(per):
                spot, row = i * per + j, block * per + j
                edge_ref[row : row + 1, cols] = got_ref[owner, spot // 4, spot % 4 : spot % 4 + 1, :]
    leaves = x_ref.shape[0] // sections
    chunks = sems.shape[1]
    each = leaves // chunks
    for chunk in range(chunks):
        for i in range(chunk * each, (chunk + 1) * each):
            rows = slice(i * sections, (i + 1) * sections)
            offset = 2 * leaves * sections + i * sections
            pick = thin_ref[offset : offset + sections, :]
            for start in range(0, nodes, LANES):
                cols = slice(start, start + LANES)
                ends = jnp.where(pick > 1.5, last_ref[:, cols], first_ref[:, cols])
                average = jnp.where(pick > 0.5, ends, own_ref[rows, cols])
                average_ref[rows, cols] = average
                new_dual_ref[rows, cols] = dual_ref[rows, cols] + penalty * (
                    x_ref[rows, cols] - average
                )
        part = pl.ds(chunk * each * sections, each * sections)
        for n, (src, dst) in enumerate(((average_ref, average_hbm), (new_dual_ref, new_dual_hbm))):
            copy = pltpu.make_async_copy(src.at[part, :], dst.at[part, :], sems.at[n, chunk])
            copy.start()
            copies.append(copy)
    for copy in copies:
        copy.wait()


def call(kernel, inputs, outputs, in_specs=None, out_specs=None, scratch=(), name=None):
    return pl.pallas_call(
        kernel,
        out_shape=outputs,
        in_specs=in_specs or [VMEM] * len(inputs),
        out_specs=out_specs or jax.tree.map(lambda _: VMEM, outputs),
        scratch_shapes=scratch,
        compiler_params=PARAMS,
        name=name,
    )(*inputs)


def shaped(shape, dtype=jnp.float32):
    return jax.ShapeDtypeStruct(shape, dtype)


def far(array):
    return pltpu.with_memory_space_constraint(array, pltpu.HBM)


def local(anchor, cost_lin, dual, target, leaf_weight, q_mat, diag_gain, block_mask, ancestor):
    leaves, sections, nodes = anchor.shape
    rows = leaves * sections
    groups = lax.axis_size("scen")
    total_nodes = lax.axis_size("feeder") * nodes
    flat = lambda a: a.reshape(rows, nodes)
    spread_shape = shaped((lax.axis_size("feeder"), 1, rows))
    full, small = shaped((rows, nodes)), shaped((4 * rows + sections + 8, LANES))
    buffer = pltpu.VMEM((rows, nodes), jnp.float32)
    edge = pltpu.VMEM((sections, nodes), jnp.float32)

    narrow = pltpu.VMEM((rows, nodes), jnp.bfloat16)
    spread = call(
        sum_kernel,
        (far(flat(anchor)),),
        spread_shape,
        in_specs=[HBM],
        scratch=(narrow, pltpu.SemaphoreType.DMA((rows // LANES,))),
        name="start_sums",
    )
    got = lax.all_to_all(spread, "feeder", 0, 0)
    first_leaf = (lax.axis_index("scen") * leaves).astype(jnp.int32).reshape(1)
    small_args = (
        target, ancestor.T, leaf_weight.reshape(1, leaves), block_mask[0],
        diag_gain.reshape(1, nodes),
    )
    large_args = (q_mat, flat(anchor), flat(cost_lin), flat(dual))
    q_eff, fixed, z, gain, thin = call(
        prep_kernel,
        (first_leaf,) + tuple(far(a) for a in small_args + large_args),
        (shaped((nodes, nodes), jnp.bfloat16), full, full, shaped((1, nodes)), small),
        in_specs=[SMEM] + [HBM] * 9,
        scratch=tuple(pltpu.VMEM(a.shape, a.dtype) for a in small_args + large_args)
        + (pltpu.SemaphoreType.DMA((9,)),),
        name="prep",
    )
    for sweep in range(PROX_ITERS - 1):
        spread, z = call(
            lambda *refs: step_kernel(total_nodes, *refs),
            (got, z, q_eff, fixed, gain),
            (spread_shape, full),
            scratch=(buffer,),
            name="prox_step",
        )
        got = lax.all_to_all(spread, "feeder", 0, 0)
    per = sections * (nodes // LANES) // groups
    x, own, sent = call(
        lambda *refs: last_kernel(total_nodes, leaves, *refs),
        (got, z, thin),
        (full, full, shaped((groups, 1, (2 * per + 1) * LANES))),
        scratch=(edge, edge),
        name="last_step",
    )
    got = lax.all_to_all(sent, "scen", 0, 0)
    back = call(owner_kernel, (got,), shaped((groups, per // 2, 4, LANES)),
                scratch=(pltpu.VMEM((groups, 16, LANES), jnp.float32),), name="owner_chain")
    got = lax.all_to_all(back, "scen", 0, 0)
    x, average, new_dual = call(
        final_kernel,
        (got, own, thin, x, flat(dual)),
        (full, full, full),
        out_specs=(HBM, HBM, HBM),
        scratch=(
            edge, edge, buffer, buffer, pltpu.SemaphoreType.DMA((2, 4)), pltpu.SemaphoreType.DMA
        ),
        name="finish",
    )
    whole = lambda a: a.reshape(leaves, sections, nodes)
    return (whole(x), whole(average), whole(new_dual))


def solution(mesh):
    return jax.shard_map(
        local,
        mesh=mesh,
        in_specs=(
            P("scen", None, "feeder"),
            P("scen", None, "feeder"),
            P("scen", None, "feeder"),
            P("scen", None),
            P("scen"),
            P("feeder", None),
            P("feeder"),
            P("feeder", None, None),
            P(None, "scen"),
        ),
        out_specs=(P("scen", None, "feeder"), P("scen", None, "feeder"), P("scen", None, "feeder")),
        check_vma=False,
    )
```

```python
import jax
import jax.numpy as jnp
from jax import lax
from jax.experimental import pallas as pl
from jax.experimental.pallas import tpu as pltpu
from jax.sharding import PartitionSpec as P

PROX_ITERS = 8
LANES = 128


penalty = 1.0
step_size = 0.08
coupling = 4.0
power_limit = 2.0

VMEM = pl.BlockSpec(memory_space=pltpu.VMEM)
SMEM = pl.BlockSpec(memory_space=pltpu.SMEM)
HBM = pl.BlockSpec(memory_space=pltpu.HBM)
PARAMS = pltpu.CompilerParams(vmem_limit_bytes=12 * 1024 * 1024)


def row_sums(block):
    total = block[:, :LANES]
    for start in range(LANES, block.shape[1], LANES):
        total = total + block[:, start : start + LANES]
    return jnp.sum(total.T, axis=0, keepdims=True)


def fetch(pairs, sems):
    copies = [pltpu.make_async_copy(src, dst, sems.at[i]) for i, (src, dst) in enumerate(pairs)]
    for copy in copies:
        copy.start()
    return copies


def sum_kernel(anchor_hbm, spread_ref, anchor_ref, sems):
    parts = [pl.ds(i * LANES, LANES) for i in range(anchor_ref.shape[0] // LANES)]
    copies = fetch([(anchor_hbm.at[part, :], anchor_ref.at[part, :]) for part in parts], sems)
    for i, part in enumerate(parts):
        copies[i].wait()
        total = row_sums(anchor_ref[part, :].astype(jnp.float32))
        for feeder in range(spread_ref.shape[0]):
            spread_ref[feeder, i : i + 1, :] = total


def affine(x, image, gain, fixed):
    return x * gain - (fixed + step_size * image)


def column(row):
    n = row.shape[1]
    down = lax.broadcasted_iota(jnp.int32, (n, n), 0)
    across = lax.broadcasted_iota(jnp.int32, (n, n), 1)
    spread = jnp.broadcast_to(row, (n, n))
    return jnp.sum(jnp.where(down == across, spread, 0.0), axis=1, keepdims=True)


def prep_kernel(
    first_ref, target_hbm, anc_hbm, weight_hbm, mask_hbm, diag_hbm,
    q_hbm, anchor_hbm, cost_hbm, dual_hbm,
    q_out, fixed_out, z_out, gain_out, thin_out,
    target_ref, anc_ref, weight_ref, mask_ref, diag_ref,
    q_ref, anchor_ref, cost_ref, dual_ref, sems,
):
    sources = (
        anc_hbm, weight_hbm, mask_hbm, diag_hbm, target_hbm, q_hbm, anchor_hbm, cost_hbm, dual_hbm
    )
    places = (
        anc_ref, weight_ref, mask_ref, diag_ref, target_ref, q_ref, anchor_ref, cost_ref, dual_ref
    )
    copies = fetch(list(zip(sources, places)), sems)
    copies[0].wait()
    copies[1].wait()
    leaves, sections = anc_ref.shape
    rows_all = leaves * sections
    thin = (sections, LANES)
    first_leaf = first_ref[0].astype(jnp.float32)
    owner_of = anc_ref[...].astype(jnp.float32)
    anc = [jnp.broadcast_to(column(owner_of[i : i + 1, :]), thin) for i in range(leaves)]
    run, same = [], []
    for i in range(leaves):
        weight = jnp.broadcast_to(weight_ref[:, i : i + 1], thin)
        thin_out[3 * rows_all + i * sections : 3 * rows_all + (i + 1) * sections, :] = weight
        same.append(jnp.where(anc[i] == anc[i - 1], 1.0, 0.0) if i else jnp.zeros(thin, jnp.float32))
        run.append(weight + same[i] * run[-1] if i else weight)
    for i in reversed(range(leaves - 1)):
        run[i] = jnp.where(same[i + 1] > 0.5, run[i + 1], run[i])
    for i in range(leaves):
        start = i * sections
        front = jnp.where(anc[i] < first_leaf, 1.0, 0.0)
        thin_out[start : start + sections, :] = same[i]
        thin_out[rows_all + start : rows_all + start + sections, :] = 1.0 / run[i]
        thin_out[2 * rows_all + start : 2 * rows_all + start + sections, :] = jnp.where(
            anc[i] == anc[-1], 2.0, front
        )
    cont = jnp.where(anc[0] < first_leaf, 1.0, 0.0)
    span = jnp.where(anc[-1] < first_leaf, 1.0, 0.0)
    end = 4 * rows_all
    thin_out[end : end + sections, :] = cont
    blocks = 8
    per = sections // 4
    section = lax.broadcasted_iota(jnp.int32, thin, 0)
    lane = lax.broadcasted_iota(jnp.int32, thin, 1)
    for block in range(4):
        place = section - block * per
        inside = (place >= 0) & (place < per)
        line = jnp.where(inside & (lane == place), run[-1], 0.0)
        line = jnp.where(inside & (lane == place + 8), run[0] * cont, line)
        line = jnp.where(inside & (lane == place + 16), span, line)
        spot = end + sections + block
        thin_out[spot : spot + 1, :] = jnp.sum(line, axis=0, keepdims=True)
    thin_out[end + sections + 4 : end + sections + blocks, :] = jnp.zeros((4, LANES), jnp.float32)
    copies[2].wait()
    copies[3].wait()
    copies[4].wait()
    gain = 1.0 - step_size * (2.0 * diag_ref[...] + penalty)
    gain_out[...] = gain

    count = mask_ref.shape[0]
    width = q_ref.shape[0] // count
    keep = mask_ref[...].astype(jnp.float32)
    copies[5].wait()
    for i in range(count):
        for j in range(count):
            rows, cols = slice(i * width, (i + 1) * width), slice(j * width, (j + 1) * width)
            block = jnp.broadcast_to(keep[i : i + 1, j : j + 1], (width, width))
            q_out[rows, cols] = q_ref[rows, cols] * block.astype(jnp.bfloat16)
    copies[6].wait()
    image = jnp.dot(anchor_ref[...], q_out[...], preferred_element_type=jnp.float32)
    z_out[...] = image
    copies[7].wait()
    copies[8].wait()
    for i in range(leaves):
        rows = slice(i * sections, (i + 1) * sections)
        pull = (step_size * coupling) * column(target_ref[i : i + 1, :])
        start_pt = anchor_ref[rows, :].astype(jnp.float32)
        linear = cost_ref[rows, :].astype(jnp.float32) + dual_ref[rows, :] - penalty * start_pt
        fixed = step_size * linear - pull
        fixed_out[rows, :] = fixed
        z_out[rows, :] = affine(start_pt, z_out[rows, :], gain, fixed)


def clipped(total_nodes, got_ref, z_ref, x_ref):
    shift = jnp.sum(got_ref[...], axis=0) * (step_size * coupling / total_nodes)
    for i in range(z_ref.shape[0] // LANES):
        rows = slice(i * LANES, (i + 1) * LANES)
        tile = jnp.broadcast_to(shift[i : i + 1, :], (LANES, LANES)).T
        for start in range(0, z_ref.shape[1], LANES):
            cols = slice(start, start + LANES)
            x_ref[rows, cols] = jnp.clip(z_ref[rows, cols] - tile, -power_limit, power_limit)


def step_kernel(
    total_nodes, got_ref, z_ref, q_ref, fixed_ref, gain_ref, sums_ref, z_out, x_ref
):
    clipped(total_nodes, got_ref, z_ref, x_ref)
    for i in range(x_ref.shape[0] // LANES):
        sums_ref[i : i + 1, :] = row_sums(x_ref[i * LANES : (i + 1) * LANES, :])
    x = x_ref[...]
    image = jnp.dot(x.astype(jnp.bfloat16), q_ref[...], preferred_element_type=jnp.float32)
    z_out[...] = affine(x, image, gain_ref[...], fixed_ref[...])


def last_kernel(
    total_nodes, leaves, got_ref, z_ref, thin_ref,
    x_ref, own_ref, sent_ref, tail_ref, head_ref,
):
    clipped(total_nodes, got_ref, z_ref, x_ref)
    rows_all, nodes = x_ref.shape
    sections = rows_all // leaves
    owners = sent_ref.shape[0]
    node_blocks = nodes // LANES
    per = sections * node_blocks // owners
    end = 4 * rows_all
    for start in range(0, nodes, LANES):
        cols = slice(start, start + LANES)
        run = []
        for i in range(leaves):
            rows = slice(i * sections, (i + 1) * sections)
            mine = slice(3 * rows_all + i * sections, 3 * rows_all + (i + 1) * sections)
            term = thin_ref[mine, :] * x_ref[rows, cols]
            run.append(term if i == 0 else term + thin_ref[rows, :] * run[-1])
        total = run[-1]
        tail_ref[:, cols] = total
        for i in reversed(range(leaves)):
            rows = slice(i * sections, (i + 1) * sections)
            if i < leaves - 1:
                later = slice((i + 1) * sections, (i + 2) * sections)
                total = jnp.where(thin_ref[later, :] > 0.5, total, run[i])
            recip = slice(rows_all + i * sections, rows_all + (i + 1) * sections)
            own_ref[rows, cols] = total * thin_ref[recip, :]
        head_ref[:, cols] = total * thin_ref[end : end + sections, :]
    for owner in range(owners):
        block, col = owner // node_blocks, owner % node_blocks
        cols = slice(col * LANES, (col + 1) * LANES)
        spot = end + sections + block
        lines = [(ref, block * per + j, cols) for ref in (tail_ref, head_ref) for j in range(per)]
        for j, (ref, row, part) in enumerate(lines + [(thin_ref, spot, slice(0, LANES))]):
            sent_ref[owner, :, j * LANES : (j + 1) * LANES] = ref[row : row + 1, part]


def owner_kernel(got_ref, back_ref, tile_ref):
    per = back_ref.shape[1] * back_ref.shape[2] // 2
    groups = got_ref.shape[0]
    shape = (8, LANES)
    for g in range(groups):
        for j in range(2 * per):
            spot = j if j < per else 8 + j - per
            tile_ref[g, spot : spot + 1, :] = got_ref[g, :, j * LANES : (j + 1) * LANES]
    zeros = jnp.zeros((8 - per, LANES), jnp.float32)
    for g in range(groups):
        tile_ref[g, per:8, :] = zeros
        tile_ref[g, 8 + per : 16, :] = zeros
    tails = [tile_ref[g, 0:8, :] for g in range(groups)]
    heads = [tile_ref[g, 8:16, :] for g in range(groups)]
    down = lax.broadcasted_iota(jnp.int32, shape, 0)
    across = lax.broadcasted_iota(jnp.int32, shape, 1)

    def scalars(g, first):
        line = jnp.broadcast_to(got_ref[g, :, 2 * per * LANES :], shape)
        mine = jnp.where(across == down + first, line, 0.0)
        return jnp.broadcast_to(jnp.sum(mine, axis=1, keepdims=True), shape)

    tail_w = [scalars(g, 0) for g in range(groups)]
    head_w = [scalars(g, 8) for g in range(groups)]
    spans = [scalars(g, 16) for g in range(groups)]
    zero = jnp.zeros(shape, jnp.float32)
    before, before_w, after, after_w = [zero], [zero], [zero], [zero]
    for g in range(groups - 1):
        before.append(tails[g] + spans[g] * before[-1])
        before_w.append(tail_w[g] + spans[g] * before_w[-1])
    for g in reversed(range(1, groups)):
        after.insert(0, heads[g] + spans[g] * after[0])
        after_w.insert(0, head_w[g] + spans[g] * after_w[0])
    for g in range(groups):
        first_w = before_w[g] + head_w[g] + spans[g] * after_w[g]
        last_w = tail_w[g] + after_w[g] + spans[g] * before_w[g]
        first_w = jnp.where(first_w > 0.0, first_w, 1.0)
        last_w = jnp.where(last_w > 0.0, last_w, 1.0)
        first = (before[g] + heads[g] + spans[g] * after[g]) / first_w
        last = (tails[g] + after[g] + spans[g] * before[g]) / last_w
        for i, row in enumerate((first, last)):
            for j in range(per):
                spot = i * per + j
                back_ref[g, spot // 4, spot % 4 : spot % 4 + 1, :] = row[j : j + 1]


def final_kernel(
    got_ref, own_ref, thin_ref, x_ref, dual_ref, x_hbm, average_hbm, new_dual_hbm,
    first_ref, last_ref, average_ref, new_dual_ref, sems, x_sem,
):
    copies = [pltpu.make_async_copy(x_ref, x_hbm, x_sem)]
    copies[0].start()
    owners = got_ref.shape[0]
    sections, nodes = first_ref.shape
    node_blocks = nodes // LANES
    per = sections * node_blocks // owners
    for owner in range(owners):
        block, col = owner // node_blocks, owner % node_blocks
        cols = slice(col * LANES, (col + 1) * LANES)
        for i, edge_ref in enumerate((first_ref, last_ref)):
            for j in range(per):
                spot, row = i * per + j, block * per + j
                edge_ref[row : row + 1, cols] = got_ref[owner, spot // 4, spot % 4 : spot % 4 + 1, :]
    leaves = x_ref.shape[0] // sections
    chunks = sems.shape[1]
    each = leaves // chunks
    for chunk in range(chunks):
        for i in range(chunk * each, (chunk + 1) * each):
            rows = slice(i * sections, (i + 1) * sections)
            offset = 2 * leaves * sections + i * sections
            pick = thin_ref[offset : offset + sections, :]
            for start in range(0, nodes, LANES):
                cols = slice(start, start + LANES)
                ends = jnp.where(pick > 1.5, last_ref[:, cols], first_ref[:, cols])
                average = jnp.where(pick > 0.5, ends, own_ref[rows, cols])
                average_ref[rows, cols] = average
                new_dual_ref[rows, cols] = dual_ref[rows, cols] + penalty * (
                    x_ref[rows, cols] - average
                )
        part = pl.ds(chunk * each * sections, each * sections)
        for n, (src, dst) in enumerate(((average_ref, average_hbm), (new_dual_ref, new_dual_hbm))):
            copy = pltpu.make_async_copy(src.at[part, :], dst.at[part, :], sems.at[n, chunk])
            copy.start()
            copies.append(copy)
    for copy in copies:
        copy.wait()


def call(kernel, inputs, outputs, in_specs=None, out_specs=None, scratch=(), name=None):
    return pl.pallas_call(
        kernel,
        out_shape=outputs,
        in_specs=in_specs or [VMEM] * len(inputs),
        out_specs=out_specs or jax.tree.map(lambda _: VMEM, outputs),
        scratch_shapes=scratch,
        compiler_params=PARAMS,
        name=name,
    )(*inputs)


def shaped(shape, dtype=jnp.float32):
    return jax.ShapeDtypeStruct(shape, dtype)


def far(array):
    return pltpu.with_memory_space_constraint(array, pltpu.HBM)


def gather_parts(part):
    spread = jnp.broadcast_to(part, (lax.axis_size("feeder"),) + part.shape)
    return lax.all_to_all(spread, "feeder", 0, 0)


def local(anchor, cost_lin, dual, target, leaf_weight, q_mat, diag_gain, block_mask, ancestor):
    leaves, sections, nodes = anchor.shape
    rows = leaves * sections
    groups = lax.axis_size("scen")
    total_nodes = lax.axis_size("feeder") * nodes
    flat = lambda a: a.reshape(rows, nodes)
    sums_shape = shaped((rows // LANES, LANES))
    full, small = shaped((rows, nodes)), shaped((4 * rows + sections + 8, LANES))
    buffer = pltpu.VMEM((rows, nodes), jnp.float32)
    edge = pltpu.VMEM((sections, nodes), jnp.float32)

    narrow = pltpu.VMEM((rows, nodes), jnp.bfloat16)
    spread = call(
        sum_kernel,
        (far(flat(anchor)),),
        shaped((lax.axis_size("feeder"),) + sums_shape.shape),
        in_specs=[HBM],
        scratch=(narrow, pltpu.SemaphoreType.DMA((rows // LANES,))),
        name="start_sums",
    )
    got = lax.all_to_all(spread, "feeder", 0, 0)
    first_leaf = (lax.axis_index("scen") * leaves).astype(jnp.int32).reshape(1)
    small_args = (
        target, ancestor.T, leaf_weight.reshape(1, leaves), block_mask[0],
        diag_gain.reshape(1, nodes),
    )
    large_args = (q_mat, flat(anchor), flat(cost_lin), flat(dual))
    q_eff, fixed, z, gain, thin = call(
        prep_kernel,
        (first_leaf,) + tuple(far(a) for a in small_args + large_args),
        (shaped((nodes, nodes), jnp.bfloat16), full, full, shaped((1, nodes)), small),
        in_specs=[SMEM] + [HBM] * 9,
        scratch=tuple(pltpu.VMEM(a.shape, a.dtype) for a in small_args + large_args)
        + (pltpu.SemaphoreType.DMA((9,)),),
        name="prep",
    )
    for sweep in range(PROX_ITERS - 1):
        sums, z = call(
            lambda *refs: step_kernel(total_nodes, *refs),
            (got, z, q_eff, fixed, gain),
            (sums_shape, full),
            scratch=(buffer,),
            name="prox_step",
        )
        got = gather_parts(sums)
    per = sections * (nodes // LANES) // groups
    x, own, sent = call(
        lambda *refs: last_kernel(total_nodes, leaves, *refs),
        (got, z, thin),
        (full, full, shaped((groups, 1, (2 * per + 1) * LANES))),
        scratch=(edge, edge),
        name="last_step",
    )
    got = lax.all_to_all(sent, "scen", 0, 0)
    back = call(owner_kernel, (got,), shaped((groups, per // 2, 4, LANES)),
                scratch=(pltpu.VMEM((groups, 16, LANES), jnp.float32),), name="owner_chain")
    got = lax.all_to_all(back, "scen", 0, 0)
    x, average, new_dual = call(
        final_kernel,
        (got, own, thin, x, flat(dual)),
        (full, full, full),
        out_specs=(HBM, HBM, HBM),
        scratch=(
            edge, edge, buffer, buffer, pltpu.SemaphoreType.DMA((2, 8)), pltpu.SemaphoreType.DMA
        ),
        name="finish",
    )
    whole = lambda a: a.reshape(leaves, sections, nodes)
    return (whole(x), whole(average), whole(new_dual))


def solution(mesh):
    return jax.shard_map(
        local,
        mesh=mesh,
        in_specs=(
            P("scen", None, "feeder"),
            P("scen", None, "feeder"),
            P("scen", None, "feeder"),
            P("scen", None),
            P("scen"),
            P("feeder", None),
            P("feeder"),
            P("feeder", None, None),
            P(None, "scen"),
        ),
        out_specs=(P("scen", None, "feeder"), P("scen", None, "feeder"), P("scen", None, "feeder")),
        check_vma=False,
    )
```
